32 devices in a mesh: gx: 4 (over y, x), gy: 8 (over z, core).
Axes of the slice: x: 2, y: 2, z: 4, core: 2. Of those that a mesh axis runs over, the one named last changes fastest.
Arguments:
- features: bfloat16 [4, 8, 512, 128], P('gx', 'gy'), may hold values from -6 to 6
- coords: float32 [4, 8, 3, 512], P('gx', 'gy'), may hold values from 0 to 1
- migrate_x_slots: int32 [4, 8, 2, 32], P('gx', 'gy'), may hold values from 0 to 511, as said below
- migrate_y_slots: int32 [4, 8, 2, 32], P('gx', 'gy'), may hold values from 0 to 511, as said below
- ghost_slots: int32 [4, 8, 256], P('gx', 'gy'), may hold values from 0 to 511, as said below
- neighbours: int32 [4, 8, 512, 16], P('gx', 'gy'), may hold values from 0 to 2815, as said below
- source_weight: bfloat16 [128, 128], replicated, may hold values from -0.5 to 0.5
- target_weight: bfloat16 [128, 128], replicated, may hold values from -0.5 to 0.5
- radial_weight: float32 [8, 128], replicated, may hold values from -2 to 2
- environ_first: bfloat16 [128, 128], replicated, may hold values from -0.5 to 0.5
- mixing_first: bfloat16 [128, 128], replicated, may hold values from -0.5 to 0.5
- coupler_first: bfloat16 [128, 128], replicated, may hold values from -0.5 to 0.5
- environ_second: bfloat16 [128, 128], replicated, may hold values from -0.5 to 0.5
- mixing_second: bfloat16 [128, 128], replicated, may hold values from -0.5 to 0.5
- coupler_second: bfloat16 [128, 128], replicated, may hold values from -0.5 to 0.5
- readout: bfloat16 [128], replicated, may hold values from -0.5 to 0.5
Outputs:
- forces: float32 [4, 8, 3, 512], P('gx', 'gy')
- energies: float32 [4, 8, 512], P('gx', 'gy')
The draws below stay inside these ranges and needn't reach their ends.
Inputs may be any that keep to these rules, and one draw needn't show every extreme that they name: `migrate_x_slots`: in each device's two rows the 64 slots are distinct. `migrate_y_slots`: in each device's two rows the 64 slots are distinct. `ghost_slots`: each device's 256 slots are distinct. `neighbours`: an entry of atom i is either a slot of the same device other than i, or 512 + s * 256 + g with s in 0..8 but never 4 and g below 256, naming ghost g of the device at grid offset (s // 3 - 1, s % 3 - 1), periodic.
All inputs are finite; a program needn't handle non-finite values.
Results may differ from the reference program's by a relative error of at most 0.005.
Values may be sent and summed in bfloat16 or wider, within the bound.
A program may use at most 64 MiB of HBM per device.

```python
import math
import jax
import jax.numpy as jnp
from jax import lax

ATOMS_DEV = 512
GHOST_DEV = 256
MIG_DEV = 32
FEATURES = 128
CHANNELS = 128
NBASIS = 8
NBRS = 16
N_GX = 4
N_GY = 8


def pick_slots(key, picked_count):
    device_total = N_GX * N_GY
    keys = jax.random.split(key, device_total)
    full = jax.vmap(lambda one_key: jax.random.permutation(one_key, ATOMS_DEV))(keys)[:, :picked_count].astype(jnp.int32)
    inner = (jax.random.permutation(jax.random.fold_in(key, 7), ATOMS_DEV - 2) + 1).astype(jnp.int32)
    leading = jnp.concatenate([jnp.array([0, ATOMS_DEV - 1], jnp.int32), inner[:picked_count - 2]])
    return full.at[0].set(leading)


def draw_migrate_x_slots(key, part):
    chosen = pick_slots(jax.random.fold_in(key, 11), 2 * MIG_DEV)
    return chosen.reshape(N_GX, N_GY, 2, MIG_DEV)


def draw_migrate_y_slots(key, part):
    chosen = pick_slots(jax.random.fold_in(key, 13), 2 * MIG_DEV)
    return chosen.reshape(N_GX, N_GY, 2, MIG_DEV)


def draw_ghost_slots(key, part):
    chosen = pick_slots(jax.random.fold_in(key, 17), GHOST_DEV)
    return chosen.reshape(N_GX, N_GY, GHOST_DEV)


def draw_neighbours(key, part):
    shape = (N_GX, N_GY, ATOMS_DEV, NBRS)
    key_owner, key_step, key_side, key_ghost = jax.random.split(jax.random.fold_in(key, 19), 4)
    owner = jax.random.randint(key_owner, shape, 0, 2)
    stride = jax.random.randint(key_step, shape, 1, ATOMS_DEV)
    self_index = jnp.arange(ATOMS_DEV, dtype=jnp.int32)[None, None, :, None]
    local_pick = (self_index + stride) % ATOMS_DEV
    block_side = jax.random.randint(key_side, shape, 0, 8)
    block_side = block_side + (block_side >= 4).astype(jnp.int32)
    ghost_pick = jax.random.randint(key_ghost, shape, 0, GHOST_DEV)
    remote = ATOMS_DEV + block_side * GHOST_DEV + ghost_pick
    chosen = jnp.where(owner == 1, local_pick, remote).astype(jnp.int32)
    chosen = chosen.at[0, 0, 0, NBRS - 1].set(ATOMS_DEV + 9 * GHOST_DEV - 1)
    chosen = chosen.at[0, 0, 1, 0].set(0)
    return chosen


def block_levels(own_key, dims, cuts, low, top_value):
    factor_of = 1.0
    for position, parts in cuts:
        heights = jax.random.uniform(jax.random.fold_in(jax.random.fold_in(own_key, 6), position), (parts,), jnp.float32, low / len(cuts), top_value / len(cuts))
        factor_of = factor_of * jnp.repeat(jnp.exp(heights), dims[position] // parts).reshape((-1,) + (1,) * (len(dims) - 1 - position))
    return factor_of


def centred(rng, dims, width, most, shards=(), held_as=jnp.bfloat16):
    result = jax.random.normal(rng, dims, jnp.float32) * width
    if len(shards) > 0:
        result = block_levels(rng, dims, shards, -0.22, 0.18) * result
    return jnp.clip(result, min=-most, max=most).astype(held_as)


def setup_inputs(seed: int = 0) -> dict:
    streams_of = jax.random.split(jax.random.key(seed), 17)
    features = centred(streams_of[0], (N_GX, N_GY, ATOMS_DEV, FEATURES), 1.0, 6.0, ((0, 4), (1, 8)))
    coords = jnp.clip(1.0 * jax.random.uniform(streams_of[1], (N_GX, N_GY, 3, ATOMS_DEV), jnp.float32) ** block_levels(streams_of[1], (N_GX, N_GY, 3, ATOMS_DEV), ((0, 4), (1, 8)), -0.2, 0.2), 0.0, 1.0)
    migrate_x_slots = draw_migrate_x_slots(jax.random.fold_in(streams_of[16], 71), 0)
    migrate_y_slots = draw_migrate_y_slots(jax.random.fold_in(streams_of[16], 71), 0)
    ghost_slots = draw_ghost_slots(jax.random.fold_in(streams_of[16], 71), 0)
    neighbours = draw_neighbours(jax.random.fold_in(streams_of[16], 71), 0)
    source_weight = centred(streams_of[6], (FEATURES, CHANNELS), FEATURES ** -0.5, 0.5)
    target_weight = centred(streams_of[7], (FEATURES, CHANNELS), FEATURES ** -0.5, 0.5)
    radial_weight = centred(streams_of[8], (NBASIS, CHANNELS), NBASIS ** -0.5, 2.0, (), jnp.float32)
    environ_first = centred(streams_of[9], (CHANNELS, CHANNELS), CHANNELS ** -0.5, 0.5)
    mixing_first = centred(streams_of[10], (CHANNELS, CHANNELS), CHANNELS ** -0.5, 0.5)
    coupler_first = centred(streams_of[11], (CHANNELS, CHANNELS), CHANNELS ** -0.5, 0.5)
    environ_second = centred(streams_of[12], (CHANNELS, CHANNELS), CHANNELS ** -0.5, 0.5)
    mixing_second = centred(streams_of[13], (CHANNELS, CHANNELS), CHANNELS ** -0.5, 0.5)
    coupler_second = centred(streams_of[14], (CHANNELS, CHANNELS), CHANNELS ** -0.5, 0.5)
    readout = centred(streams_of[15], (CHANNELS,), CHANNELS ** -0.5, 0.5)
    return dict(features=features, coords=coords, migrate_x_slots=migrate_x_slots, migrate_y_slots=migrate_y_slots, ghost_slots=ghost_slots, neighbours=neighbours, source_weight=source_weight, target_weight=target_weight, radial_weight=radial_weight, environ_first=environ_first, mixing_first=mixing_first, coupler_first=coupler_first, environ_second=environ_second, mixing_second=mixing_second, coupler_second=coupler_second, readout=readout)


soften = 0.25
cutoff = 2.0

def block_energy(positions, first_row, neighbour_block, source_block, target_table, radial_weight, layers, readout):
    block_rows, slots_per = neighbour_block.shape
    breadth = target_table.shape[1]
    flat_index = neighbour_block.reshape(block_rows * slots_per)
    pos_own = lax.dynamic_slice_in_dim(positions, first_row, block_rows, 1)
    pos_far = jnp.take(positions, flat_index, axis=1).reshape(3, block_rows, slots_per)
    offset = pos_far - pos_own[:, :, None]
    length = jnp.sqrt(lax.optimization_barrier(jnp.sum(offset * offset, axis=0)) + soften)
    direction = offset / length[None]
    scaled = length / cutoff
    smooth = (1.0 - scaled * scaled) ** 2
    frequency = (jnp.arange(radial_weight.shape[0]) + 1).astype(jnp.float32) * math.pi
    bessel = jnp.sin(scaled[:, :, None] * frequency) / length[:, :, None] * smooth[:, :, None]
    radial = jnp.einsum('rnb,bc->rnc', bessel, radial_weight, precision=lax.Precision.HIGHEST)
    gathered = jnp.take(target_table, flat_index, axis=0).reshape(block_rows, slots_per, breadth)
    paired = source_block.astype(jnp.float32)[:, None, :] + gathered.astype(jnp.float32) + radial
    hidden = jax.nn.silu(paired).reshape(block_rows * slots_per, breadth).astype(jnp.bfloat16)
    weighted = direction * smooth[None]
    norm_scale = 1.0 / math.sqrt(slots_per)
    latent = None
    for environ, mixing, coupler in layers:
        carried = jnp.dot(hidden, environ, preferred_element_type=jnp.float32).reshape(block_rows, slots_per, breadth)
        environment = [lax.optimization_barrier(jnp.sum(weighted[k][:, :, None] * carried, axis=1)) for k in range(3)]
        coupled = direction[0][:, :, None] * environment[0][:, None, :]
        coupled = coupled + direction[1][:, :, None] * environment[1][:, None, :]
        coupled = coupled + direction[2][:, :, None] * environment[2][:, None, :]
        coupled = (coupled * norm_scale).reshape(block_rows * slots_per, breadth).astype(jnp.bfloat16)
        mixed = jnp.dot(hidden, mixing, preferred_element_type=jnp.float32) + jnp.dot(coupled, coupler, preferred_element_type=jnp.float32)
        latent = jax.nn.silu(mixed)
        hidden = latent.astype(jnp.bfloat16)
    edge_energy = lax.optimization_barrier(jnp.sum(latent * readout.astype(jnp.float32)[None, :], axis=1)).reshape(block_rows, slots_per) * smooth
    atom_energy = lax.optimization_barrier(jnp.sum(edge_energy, axis=1))
    return (jnp.sum(atom_energy), atom_energy)

def device_forces(positions, neighbours, source_rows, target_table, radial_weight, layers, readout):
    atom_count = neighbours.shape[0]
    block_atoms = math.gcd(atom_count, 256)
    block_count = atom_count // block_atoms

    def advance(total, block_number):
        first_row = block_number * block_atoms
        neighbour_block = lax.dynamic_slice_in_dim(neighbours, first_row, block_atoms, 0)
        source_block = lax.dynamic_slice_in_dim(source_rows, first_row, block_atoms, 0)

        def energy_of(table_pos):
            return block_energy(table_pos, first_row, neighbour_block, source_block, target_table, radial_weight, layers, readout)
        gradient, atom_energy = jax.grad(energy_of, has_aux=True)(positions)
        return (total + gradient, atom_energy)
    total, energies = lax.scan(advance, jnp.zeros(positions.shape, jnp.float32), jnp.arange(block_count, dtype=jnp.int32))
    return (total, energies.reshape(atom_count))

def take_rows(table, picks):
    return table[picks]

def take_columns(table, picks):
    return table[:, picks]

def put_rows(table, picks, values):
    return table.at[picks].set(values)

def put_columns(table, picks, values):
    return table.at[:, picks].set(values)

def add_columns(table, picks, values):
    return table.at[:, picks].add(values)

def migrate(features, coords, slots, axis_number):
    grid_take_rows = jax.vmap(jax.vmap(take_rows))
    grid_take_cols = jax.vmap(jax.vmap(take_columns))
    grid_put_rows = jax.vmap(jax.vmap(put_rows))
    grid_put_cols = jax.vmap(jax.vmap(put_columns))
    plus_rows = grid_take_rows(features, slots[:, :, 0])
    minus_rows = grid_take_rows(features, slots[:, :, 1])
    plus_cols = grid_take_cols(coords, slots[:, :, 0])
    minus_cols = grid_take_cols(coords, slots[:, :, 1])
    features = grid_put_rows(features, slots[:, :, 0], jnp.roll(plus_rows, 1, axis=axis_number))
    features = grid_put_rows(features, slots[:, :, 1], jnp.roll(minus_rows, -1, axis=axis_number))
    coords = grid_put_cols(coords, slots[:, :, 0], jnp.roll(plus_cols, 1, axis=axis_number))
    coords = grid_put_cols(coords, slots[:, :, 1], jnp.roll(minus_cols, -1, axis=axis_number))
    return (features, coords)

def reference(features, coords, migrate_x_slots, migrate_y_slots, ghost_slots, neighbours, source_weight, target_weight, radial_weight, environ_first, mixing_first, coupler_first, environ_second, mixing_second, coupler_second, readout):
    features, coords = migrate(features, coords, migrate_x_slots, 0)
    features, coords = migrate(features, coords, migrate_y_slots, 1)
    ghost_rows = jax.vmap(jax.vmap(take_rows))(features, ghost_slots)
    ghost_coords = jax.vmap(jax.vmap(take_columns))(coords, ghost_slots)
    layers = ((environ_first, mixing_first, coupler_first), (environ_second, mixing_second, coupler_second))
    atom_count = features.shape[2]
    ghost_count = ghost_slots.shape[2]

    def one_device(flat_id):
        grid_x = flat_id // N_GY
        grid_y = flat_id % N_GY
        own_rows = features[grid_x, grid_y]
        own_coords = coords[grid_x, grid_y]
        row_parts = [own_rows]
        coord_parts = [own_coords]
        for shift_a in range(3):
            for shift_b in range(3):
                near_x = (grid_x + shift_a - 1 + N_GX) % N_GX
                near_y = (grid_y + shift_b - 1 + N_GY) % N_GY
                row_parts.append(ghost_rows[near_x, near_y])
                coord_parts.append(ghost_coords[near_x, near_y])
        table_rows = jnp.concatenate(row_parts, axis=0)
        positions = jnp.concatenate(coord_parts, axis=1)
        source_rows = jnp.dot(own_rows, source_weight, preferred_element_type=jnp.float32).astype(jnp.bfloat16)
        target_table = jnp.dot(table_rows, target_weight, preferred_element_type=jnp.float32).astype(jnp.bfloat16)
        return device_forces(positions, neighbours[grid_x, grid_y], source_rows, target_table, radial_weight, layers, readout)
    gradients, energies = lax.map(one_device, jnp.arange(N_GX * N_GY, dtype=jnp.int32))
    gradients = gradients.reshape(N_GX, N_GY, 3, atom_count + 9 * ghost_count)
    local_part = gradients[:, :, :, :atom_count]
    ghost_part = gradients[:, :, :, atom_count:].reshape(N_GX, N_GY, 3, 3, 3, ghost_count)
    returned = jnp.zeros((N_GX, N_GY, 3, ghost_count), jnp.float32)
    for shift_a in range(3):
        for shift_b in range(3):
            returned = returned + jnp.roll(ghost_part[:, :, :, shift_a, shift_b], (shift_a - 1, shift_b - 1), axis=(0, 1))
    total = jax.vmap(jax.vmap(add_columns))(local_part, ghost_slots, returned)
    return (-total, energies.reshape(N_GX, N_GY, atom_count))
```

```python
import functools
import math

import jax
import jax.numpy as jnp
from jax import lax
from jax.experimental import pallas as pl
from jax.experimental.pallas import tpu as pltpu
from jax.sharding import PartitionSpec as P

soften = 0.25
cutoff = 2.0


def split_three(value):
    top = value.astype(jnp.bfloat16).astype(jnp.float32)
    rest = value - top
    middle = rest.astype(jnp.bfloat16).astype(jnp.float32)
    return (top, middle, rest - middle)


def sigmoid(value):
    return 0.5 * jnp.tanh(0.5 * value) + 0.5


def turned(weight):
    return weight.astype(jnp.float32).T.astype(jnp.bfloat16)


def edge_kernel(
    block_atoms,
    index_ref,
    table_ref,
    source_ref,
    place_ref,
    own_ref,
    radial_far,
    environ_first_far,
    mixing_first_far,
    coupler_first_far,
    environ_second_far,
    mixing_second_far,
    coupler_second_far,
    readout_far,
    scatter_ref,
    atom_ref,
    energy_ref,
    radial_ref,
    environ_first,
    mixing_first,
    coupler_first,
    environ_second,
    mixing_second,
    coupler_second,
    readout_ref,
    fetch_sem,
    index_sem,
    index_smem,
    gathered,
    scalars,
    results,
    saved,
    forward_weights,
    backward_weights,
    environ_turned,
    radial_in,
    radial_out,
    pick_weights,
    place_split,
):
    slots_per, atom_count = index_ref.shape
    breadth = table_ref.shape[1]
    groups = place_ref.shape[1]
    f32 = jnp.float32
    bf16 = jnp.bfloat16
    lists = [
        pltpu.make_async_copy(
            index_ref.at[slot],
            index_smem.at[pl.ds(slot * atom_count, atom_count)],
            index_sem.at[slot],
        )
        for slot in range(slots_per)
    ]
    for fetch in lists:
        fetch.start()
    fetches = [
        pltpu.make_async_copy(far, near, fetch_sem.at[n])
        for n, (far, near) in enumerate(
            (
                (radial_far, radial_ref),
                (environ_first_far, environ_first),
                (mixing_first_far, mixing_first),
                (coupler_first_far, coupler_first),
                (environ_second_far, environ_second),
                (mixing_second_far, mixing_second),
                (coupler_second_far, coupler_second),
                (readout_far, readout_ref),
            )
        )
    ]
    for fetch in fetches:
        fetch.start()

    for fetch in lists:
        fetch.wait()
    step = math.gcd(atom_count, 16)

    @pl.loop(0, slots_per)
    def _(slot):
        @pl.loop(0, atom_count // step)
        def _(part):
            base = pl.multiple_of(part * step, step)
            start = slot * atom_count + base
            for u in range(step):
                row = index_smem[start + u]
                gathered[slot, pl.ds(base + u, 1), :] = table_ref[pl.ds(row, 1), :]

    for fetch in fetches:
        fetch.wait()

    forward_weights[0, :, :breadth] = environ_first[...]
    forward_weights[0, :, breadth:] = mixing_first[...]
    forward_weights[1, :, :breadth] = environ_second[...]
    forward_weights[1, :, breadth:] = mixing_second[...]
    backward_weights[0, :, :breadth] = turned(coupler_first[...])
    backward_weights[0, :, breadth:] = turned(mixing_first[...])
    backward_weights[1, :, :breadth] = turned(coupler_second[...])
    backward_weights[1, :, breadth:] = turned(mixing_second[...])
    environ_turned[0] = turned(environ_first[...])
    environ_turned[1] = turned(environ_second[...])
    w_top, w_mid, w_low = split_three(radial_ref[...])
    basis = radial_ref.shape[0]
    lead = jnp.zeros((8, breadth), f32)
    tail = jnp.zeros((breadth - 8 - 6 * basis, breadth), f32)
    radial_in[...] = jnp.concatenate(
        [lead, w_top, w_mid, w_low, w_top, w_mid, w_top, tail], axis=0
    ).astype(bf16)
    wide = jnp.concatenate(
        [lead, w_top, w_mid, jnp.zeros((breadth - 8 - 2 * basis, breadth), f32)], axis=0
    ).T.astype(bf16)
    radial_out[:breadth, :] = wide
    radial_out[breadth:, :] = wide
    lane_id = lax.broadcasted_iota(jnp.int32, (breadth, breadth), 1)
    for k in range(4):
        pick_weights[k * breadth : (k + 1) * breadth, :] = (
            jnp.where(lane_id == k, 1.0, 0.0).astype(bf16)
        )
    places = place_ref[...].reshape(3 * groups, breadth)
    p_top, p_mid, p_low = split_three(places)
    place_split[...] = jnp.concatenate([p_top, p_mid, p_low], axis=0).astype(bf16)

    def chosen(slot):
        index = index_ref[pl.ds(slot, 1), :]
        low = lax.rem(index, breadth)
        high = lax.div(index, breadth)
        rows = lax.broadcasted_iota(jnp.int32, (breadth, atom_count), 0)
        one_hot = jnp.where(rows == low, 1.0, 0.0).astype(bf16)
        group_rows = lax.broadcasted_iota(jnp.int32, (groups, atom_count), 0)
        return (one_hot, group_rows == high)

    @pl.loop(0, slots_per, unroll=4)
    def _(slot):
        one_hot, in_group = chosen(slot)
        found = jnp.dot(place_split[...], one_hot, preferred_element_type=f32)
        size = 3 * groups
        found = found[:size] + found[size : 2 * size] + found[2 * size :]
        offsets = []
        for k in range(3):
            far = jnp.sum(
                jnp.where(in_group, found[k * groups : (k + 1) * groups], 0.0),
                axis=0,
                keepdims=True,
            )
            offsets.append(far - own_ref[k : k + 1, :])
        square = offsets[0] * offsets[0] + offsets[1] * offsets[1] + offsets[2] * offsets[2]
        length = jnp.sqrt(square + soften)
        inverse = 1.0 / length
        scaled = length / cutoff
        smooth = (1.0 - scaled * scaled) ** 2
        angle = scaled * math.pi
        sine = jnp.sin(angle)
        cosine = jnp.cos(angle)
        factor = inverse * smooth
        before, now = (jnp.zeros_like(sine), sine)
        waves = []
        for _ in range(basis):
            waves.append(now * factor)
            before, now = (now, 2.0 * cosine * now - before)
        bessel = jnp.concatenate(waves, axis=0)
        b_top, b_mid, b_low = split_three(bessel)
        blank = jnp.zeros_like(sine)
        head = [offsets[k] * inverse for k in range(3)] + [smooth] + [blank] * 4
        spare = jnp.zeros((breadth - 8 - 6 * basis, atom_count), f32)
        stack = jnp.concatenate(
            head + [b_top, b_top, b_top, b_mid, b_mid, b_low, spare], axis=0
        )
        scalars[slot] = stack.T
        saved[slot] = jnp.concatenate(offsets + [length, sine, cosine, blank, blank], axis=0)

    norm_scale = 1.0 / math.sqrt(slots_per)
    edges = slots_per * block_atoms
    cube = (slots_per, block_atoms, breadth)
    readout_row = readout_ref[...].astype(f32)[None]
    couplers = (coupler_first, coupler_second)
    ee_lane = lax.broadcasted_iota(jnp.int32, (edges, breadth), 1) == 4

    def product(left, right):
        return jnp.dot(left.astype(bf16), right, preferred_element_type=f32)

    @pl.loop(0, atom_count // block_atoms, unroll=1)
    def _(block):
        first = pl.multiple_of(block * block_atoms, block_atoms)
        atoms = pl.ds(first, block_atoms)
        narrow = scalars[:, atoms, :]
        radial = product(narrow.reshape(edges, breadth), radial_in[...]).reshape(cube)
        rows = gathered[:, atoms, :]
        paired = rows + source_ref[atoms, :][None] + radial
        gate = sigmoid(paired)
        value = paired * gate
        slopes = [gate + value * (1.0 - gate)]
        hidden = value.reshape(edges, breadth).astype(bf16)
        direction = [jnp.broadcast_to(narrow[:, :, k : k + 1], cube) for k in range(3)]
        smooth = jnp.broadcast_to(narrow[:, :, 3:4], cube)
        kept = []
        for layer in range(2):
            both = jnp.dot(hidden, forward_weights[layer], preferred_element_type=f32)
            carried = both[:, :breadth].reshape(cube)
            eased = smooth * carried
            environment = [
                jnp.sum(direction[k] * eased, axis=0) * norm_scale for k in range(3)
            ]
            coupled = direction[0] * environment[0][None]
            coupled = coupled + direction[1] * environment[1][None]
            coupled = coupled + direction[2] * environment[2][None]
            mixed = both[:, breadth:] + product(
                coupled.reshape(edges, breadth), couplers[layer][...]
            )
            mixed = mixed.reshape(cube)
            gate = sigmoid(mixed)
            value = mixed * gate
            slopes.append(gate + value * (1.0 - gate))
            kept.append((carried, eased, environment))
            if layer == 0:
                hidden = value.reshape(edges, breadth).astype(bf16)
        edge_energy = jnp.sum(value * readout_row, axis=2, keepdims=True)
        flow = smooth * readout_row
        sums = None
        for layer in (1, 0):
            carried, eased, environment = kept[layer]
            mixed_grad = flow * slopes[layer + 1]
            back = product(mixed_grad.reshape(edges, breadth), backward_weights[layer])
            coupled_grad = back[:, :breadth].reshape(cube)
            environment_grad = [
                jnp.sum(direction[k] * coupled_grad, axis=0) * norm_scale for k in range(3)
            ]
            spread = direction[0] * environment_grad[0][None]
            spread = spread + direction[1] * environment_grad[1][None]
            spread = spread + direction[2] * environment_grad[2][None]
            parts = [
                coupled_grad * environment[k][None] + eased * environment_grad[k][None]
                for k in range(3)
            ] + [carried * spread]
            sums = parts if sums is None else [x + y for x, y in zip(sums, parts)]
            flow = back[:, breadth:].reshape(cube) + product(
                (smooth * spread).reshape(edges, breadth), environ_turned[layer]
            ).reshape(cube)
        paired_grad = (flow * slopes[0]).reshape(edges, breadth)
        high = paired_grad.astype(bf16)
        low = (paired_grad - high.astype(f32)).astype(bf16)
        total = jnp.dot(
            jnp.concatenate([high, low], axis=1), radial_out[...], preferred_element_type=f32
        )
        total = total + jnp.dot(
            jnp.concatenate([x.reshape(edges, breadth).astype(bf16) for x in sums], axis=1),
            pick_weights[...],
            preferred_element_type=f32,
        )
        total = jnp.where(
            ee_lane, jnp.broadcast_to(edge_energy, cube).reshape(edges, breadth), total
        )
        results[:, atoms, :] = total.reshape(cube)

    scatter_ref[...] = jnp.zeros(scatter_ref.shape, f32)
    atom_ref[...] = jnp.zeros(atom_ref.shape, f32)
    energy_ref[...] = jnp.zeros(energy_ref.shape, f32)

    @pl.loop(0, slots_per, unroll=1)
    def _(slot):
        flat = results[slot].T
        data = saved[slot]
        offsets = [data[k : k + 1] for k in range(3)]
        length, sine, cosine = (data[3:4], data[4:5], data[5:6])
        inverse = 1.0 / length
        scaled = length / cutoff
        under = 1.0 - scaled * scaled
        smooth = under * under
        direction = [offsets[k] * inverse for k in range(3)]
        sin_before, sin_now = (jnp.zeros_like(sine), sine)
        cos_before, cos_now = (jnp.ones_like(sine), cosine)
        first_sum = jnp.zeros_like(sine)
        second_sum = jnp.zeros_like(sine)
        for b in range(basis):
            grad = flat[8 + b : 9 + b] + flat[8 + basis + b : 9 + basis + b]
            first_sum = first_sum + grad * sin_now
            second_sum = second_sum + grad * (cos_now * ((b + 1) * math.pi / cutoff))
            sin_before, sin_now = (sin_now, 2.0 * cosine * sin_now - sin_before)
            cos_before, cos_now = (cos_now, 2.0 * cosine * cos_now - cos_before)
        edge_energy = flat[4:5]
        smooth_grad = flat[3:4] + edge_energy + first_sum * inverse
        along = flat[0:1] * direction[0] + flat[1:2] * direction[1] + flat[2:3] * direction[2]
        length_grad = smooth * inverse * (second_sum - first_sum * inverse)
        length_grad = length_grad - smooth_grad * under * (2.0 * scaled / cutoff) * 2.0
        length_grad = length_grad - along * inverse
        one_hot, in_group = chosen(slot)
        pieces = []
        atom_rows = []
        for k in range(3):
            grad = flat[k : k + 1] * inverse + length_grad * direction[k]
            atom_rows.append(-grad)
            pieces.append(jnp.where(in_group, jnp.broadcast_to(grad, in_group.shape), 0.0))
        spread = jnp.concatenate(pieces, axis=0)
        top = spread.astype(bf16)
        low = (spread - top.astype(f32)).astype(bf16)
        for piece in (top, low):
            scatter_ref[...] += lax.dot_general(
                piece, one_hot, (((1,), (1,)), ((), ())), preferred_element_type=f32
            )
        blank = jnp.zeros_like(sine)
        atom_ref[...] += jnp.concatenate(atom_rows + [blank] * 5, axis=0)
        energy_ref[...] += edge_energy * smooth


def others(shape):
    here = (lax.axis_index("gx"), lax.axis_index("gy"))
    steps = [(n // 3 - 1, n % 3 - 1) for n in range(9)]

    def at(dx, dy):
        return (
            lax.rem(here[0] + (dx + shape[0]), shape[0]),
            lax.rem(here[1] + (dy + shape[1]), shape[1]),
        )

    return (at, steps)


def greet(shape):
    at, steps = others(shape)
    barrier = pltpu.get_barrier_semaphore()
    for dx, dy in steps:
        if (dx, dy) != (0, 0):
            pl.semaphore_signal(
                barrier, inc=1, device_id=at(dx, dy), device_id_type=pl.DeviceIdType.MESH
            )
    return barrier


def hot_columns(slots, count):
    rows = lax.broadcasted_iota(jnp.int32, (count, slots.shape[1]), 0)
    return jnp.where(rows == slots, 1.0, 0.0)


def share_kernel(
    shape,
    features_far,
    coords,
    slots_x_far,
    slots_y_far,
    ghosts_far,
    source_weight_far,
    target_weight_far,
    table_ref,
    source_ref,
    place_ref,
    own_ref,
    features,
    slots_x,
    slots_y,
    ghosts,
    source_weight,
    target_weight,
    fetch_sem,
    holding,
    leaving,
    arriving,
    ghost_rows,
    ghost_places,
    halo_rows,
    halo_places,
    move_send,
    move_recv,
    rows_send,
    rows_recv,
    places_send,
    places_recv,
):
    f32 = jnp.float32
    bf16 = jnp.bfloat16
    mesh_ids = pl.DeviceIdType.MESH
    count, breadth = features.shape
    sent = slots_x.shape[1]
    ghost_count = ghosts.shape[1]
    at, steps = others(shape)
    barrier = greet(shape)
    fetches = [
        pltpu.make_async_copy(far, near, fetch_sem.at[n])
        for n, (far, near) in enumerate(
            (
                (features_far, features),
                (slots_x_far, slots_x),
                (slots_y_far, slots_y),
                (ghosts_far, ghosts),
                (source_weight_far, source_weight),
                (target_weight_far, target_weight),
            )
        )
    ]
    for fetch in fetches:
        fetch.start()

    blank = jnp.zeros((5, count), f32)
    pieces = []
    for piece in split_three(coords[...].reshape(3, count)):
        pieces += [piece, blank]
    pieces.append(jnp.zeros((breadth - 24, count), f32))
    holding[:, breadth:] = jnp.concatenate(pieces, axis=0).T.astype(bf16)
    for fetch in fetches:
        fetch.wait()
    holding[:, :breadth] = features[...]
    slots_x = jnp.concatenate([slots_x[0:1, :], slots_x[1:2, :]], axis=1)
    slots_y = jnp.concatenate([slots_y[0:1, :], slots_y[1:2, :]], axis=1)
    both = jnp.concatenate([slots_x, slots_y], axis=1)
    picks = hot_columns(both, count).T.astype(bf16)
    ghost_hot = hot_columns(ghosts[...], count)
    ghost_picks = ghost_hot.T.astype(bf16)
    ghost_hot = ghost_hot.astype(bf16)

    for axis, slots in ((0, slots_x), (1, slots_y)):
        chosen = picks[2 * sent * axis : 2 * sent * (axis + 1)]
        payload = jnp.dot(chosen, holding[...], preferred_element_type=f32).astype(bf16)
        leaving[axis, 0] = payload[:sent]
        leaving[axis, 1] = payload[sent:]
        put = hot_columns(slots, count)
        hit = jnp.max(put, axis=1, keepdims=True) > 0.5
        put = put.astype(bf16)
        if axis == 0:
            pl.semaphore_wait(barrier, 8)
        copies = []
        for way, stride in ((0, 1), (1, -1)):
            copy = pltpu.make_async_remote_copy(
                src_ref=leaving.at[axis, way],
                dst_ref=arriving.at[axis, way],
                send_sem=move_send.at[axis, way],
                recv_sem=move_recv.at[axis, way],
                device_id=at(stride, 0) if axis == 0 else at(0, stride),
                device_id_type=mesh_ids,
            )
            copy.start()
            copies.append(copy)
        for copy in copies:
            copy.wait()
        came = arriving[axis].reshape(2 * sent, 2 * breadth)
        moved = jnp.dot(put, came, preferred_element_type=f32)
        holding[...] = jnp.where(hit, moved, holding[...].astype(f32)).astype(bf16)

    rows = holding[:, :breadth]
    target = jnp.dot(rows, target_weight[...], preferred_element_type=f32).astype(bf16)
    ghost_rows[...] = jnp.dot(ghost_picks, target, preferred_element_type=f32).astype(bf16)
    flat = holding[:, breadth:].astype(f32).T[:24]
    ghost_flat = jnp.dot(flat.astype(bf16), ghost_hot, preferred_element_type=f32)
    ghost_places[...] = ghost_flat[:8] + ghost_flat[8:16] + ghost_flat[16:24]
    copies = {}
    for n, (dx, dy) in enumerate(steps):
        if (dx, dy) == (0, 0):
            continue
        copies[n] = []
        for source, landing, send, recv in (
            (ghost_places, halo_places, places_send, places_recv),
            (ghost_rows, halo_rows, rows_send, rows_recv),
        ):
            copy = pltpu.make_async_remote_copy(
                src_ref=source,
                dst_ref=landing.at[n],
                send_sem=send.at[n],
                recv_sem=recv.at[n],
                device_id=at(-dx, -dy),
                device_id_type=mesh_ids,
            )
            copy.start()
            copies[n].append(copy)
    table_ref[:count, :] = target.astype(f32)
    source_ref[...] = (
        jnp.dot(rows, source_weight[...], preferred_element_type=f32).astype(bf16).astype(f32)
    )
    mine = flat[:8] + flat[8:16] + flat[16:24]
    own_ref[...] = mine
    place_ref[...] = jnp.zeros(place_ref.shape, f32)
    own_groups = count // breadth
    for k in range(3):
        for g in range(own_groups):
            place_ref[k, g : g + 1, :] = mine[k : k + 1, g * breadth : (g + 1) * breadth]
    ghost_groups = ghost_count // breadth
    for n in range(9):
        rows_at = pl.ds(count + n * ghost_count, ghost_count)
        if n not in copies:
            table_ref[rows_at, :] = jnp.zeros((ghost_count, breadth), f32)
            continue
        for copy in copies[n]:
            copy.wait()
        table_ref[rows_at, :] = halo_rows[n].astype(f32)
        places = halo_places[n]
        for k in range(3):
            for g in range(ghost_groups):
                group = own_groups + n * ghost_groups + g
                place_ref[k, group : group + 1, :] = places[
                    k : k + 1, g * breadth : (g + 1) * breadth
                ]


def return_kernel(
    shape, scattered, by_atom, ghosts, force_ref, leaving, arriving, send_sem, recv_sem
):
    f32 = jnp.float32
    bf16 = jnp.bfloat16
    count = by_atom.shape[1]
    breadth = scattered.shape[1]
    groups = scattered.shape[0] // 3
    ghost_groups = ghosts.shape[1] // breadth
    own_groups = count // breadth
    at, steps = others(shape)
    blank = jnp.zeros((5, breadth), f32)
    for n in range(9):
        for g in range(ghost_groups):
            group = own_groups + n * ghost_groups + g
            piece = [scattered[pl.ds(k * groups + group, 1), :] for k in range(3)]
            leaving[n, :, g * breadth : (g + 1) * breadth] = jnp.concatenate(
                piece + [blank], axis=0
            )
    spots = hot_columns(ghosts[...], count).T.astype(bf16)
    copies = []
    for n, (dx, dy) in enumerate(steps):
        if (dx, dy) == (0, 0):
            continue
        copy = pltpu.make_async_remote_copy(
            src_ref=leaving.at[n],
            dst_ref=arriving.at[n],
            send_sem=send_sem.at[n],
            recv_sem=recv_sem.at[n],
            device_id=at(dx, dy),
            device_id_type=pl.DeviceIdType.MESH,
        )
        copy.start()
        copies.append((n, copy))
    total = leaving[4]
    for n, copy in copies:
        copy.wait()
        total = total + arriving[n]
    stack = jnp.concatenate(split_three(total), axis=0).astype(bf16)
    back = jnp.dot(stack, spots, preferred_element_type=f32)
    back = back[:8] + back[8:16] + back[16:24]
    for k in range(3):
        own = jnp.concatenate(
            [scattered[pl.ds(k * groups + g, 1), :] for g in range(own_groups)], axis=1
        )
        force_ref[k] = -(own + by_atom[k : k + 1, :] + back[k : k + 1, :])


def whole_kernel(
    shape,
    block_atoms,
    features_far,
    coords,
    slots_x_far,
    slots_y_far,
    ghosts_far,
    neighbours,
    source_weight_far,
    target_weight_far,
    radial_far,
    environ_first_far,
    mixing_first_far,
    coupler_first_far,
    environ_second_far,
    mixing_second_far,
    coupler_second_far,
    readout_far,
    force_ref,
    energy_ref,
    table_ref,
    source_ref,
    place_ref,
    own_ref,
    scatter_ref,
    atom_ref,
    *scratch,
):
    share, edge, back = scratch[:20], scratch[20:42], scratch[42:]
    ghosts = share[3]
    share_kernel(
        shape,
        features_far,
        coords,
        slots_x_far,
        slots_y_far,
        ghosts_far,
        source_weight_far,
        target_weight_far,
        table_ref,
        source_ref,
        place_ref,
        own_ref,
        *share,
    )
    edge_kernel(
        block_atoms,
        neighbours,
        table_ref,
        source_ref,
        place_ref,
        own_ref,
        radial_far,
        environ_first_far,
        mixing_first_far,
        coupler_first_far,
        environ_second_far,
        mixing_second_far,
        coupler_second_far,
        readout_far,
        scatter_ref,
        atom_ref,
        energy_ref,
        *edge,
    )
    return_kernel(shape, scatter_ref, atom_ref, ghosts, force_ref, *back)


def per_device(
    shape,
    features,
    coords,
    migrate_x_slots,
    migrate_y_slots,
    ghost_slots,
    neighbours,
    source_weight,
    target_weight,
    radial_weight,
    environ_first,
    mixing_first,
    coupler_first,
    environ_second,
    mixing_second,
    coupler_second,
    readout,
):
    features = features[0, 0]
    count, breadth = features.shape
    coords = coords.transpose(0, 2, 1, 3).reshape(3, 1, count)
    neighbours = neighbours[0, 0].T
    ghosts = ghost_slots.reshape(1, -1)
    slots_per = neighbours.shape[0]
    ghost_count = ghosts.shape[1]
    sent = migrate_x_slots.shape[3]
    total_rows = count + 9 * ghost_count
    groups = -(-(total_rows // breadth) // 8) * 8
    f32 = jnp.float32
    bf16 = jnp.bfloat16
    vmem = pl.BlockSpec(memory_space=pltpu.VMEM)
    hbm = pl.BlockSpec(memory_space=pltpu.HBM)
    dma = pltpu.SemaphoreType.DMA
    block_atoms = math.gcd(count, 64)
    cube = (slots_per, count, breadth)
    forces, energies = pl.pallas_call(
        functools.partial(whole_kernel, shape, block_atoms),
        out_shape=(
            jax.ShapeDtypeStruct((3, 1, count), f32),
            jax.ShapeDtypeStruct((1, count), f32),
        ),
        in_specs=[hbm, vmem, hbm, hbm, hbm, vmem] + [hbm] * 10,
        out_specs=(vmem,) * 2,
        scratch_shapes=[
            pltpu.VMEM((total_rows, breadth), f32),
            pltpu.VMEM((count, breadth), f32),
            pltpu.VMEM((3, groups, breadth), f32),
            pltpu.VMEM((8, count), f32),
            pltpu.VMEM((3 * groups, breadth), f32),
            pltpu.VMEM((8, count), f32),
            pltpu.VMEM((count, breadth), bf16),
            pltpu.VMEM((2, sent), jnp.int32),
            pltpu.VMEM((2, sent), jnp.int32),
            pltpu.VMEM((1, ghost_count), jnp.int32),
            pltpu.VMEM((breadth, breadth), bf16),
            pltpu.VMEM((breadth, breadth), bf16),
            dma((6,)),
            pltpu.VMEM((count, 2 * breadth), bf16),
            pltpu.VMEM((2, 2, sent, 2 * breadth), bf16),
            pltpu.VMEM((2, 2, sent, 2 * breadth), bf16),
            pltpu.VMEM((ghost_count, breadth), bf16),
            pltpu.VMEM((8, ghost_count), f32),
            pltpu.VMEM((9, ghost_count, breadth), bf16),
            pltpu.VMEM((9, 8, ghost_count), f32),
            dma((2, 2)),
            dma((2, 2)),
            dma((9,)),
            dma((9,)),
            dma((9,)),
            dma((9,)),
            pltpu.VMEM(radial_weight.shape, f32),
        ]
        + [pltpu.VMEM((breadth, breadth), bf16)] * 6
        + [
            pltpu.VMEM((1, breadth), bf16),
            dma((8,)),
            dma((slots_per,)),
            pltpu.SMEM((slots_per * count,), jnp.int32),
            pltpu.VMEM(cube, f32),
            pltpu.VMEM(cube, f32),
            pltpu.VMEM(cube, f32),
            pltpu.VMEM((slots_per, 8, count), f32),
            pltpu.VMEM((2, breadth, 2 * breadth), bf16),
            pltpu.VMEM((2, breadth, 2 * breadth), bf16),
            pltpu.VMEM((2, breadth, breadth), bf16),
            pltpu.VMEM((breadth, breadth), bf16),
            pltpu.VMEM((2 * breadth, breadth), bf16),
            pltpu.VMEM((4 * breadth, breadth), bf16),
            pltpu.VMEM((9 * groups, breadth), bf16),
            pltpu.VMEM((9, 8, ghost_count), f32),
            pltpu.VMEM((9, 8, ghost_count), f32),
            dma((9,)),
            dma((9,)),
        ],
        compiler_params=pltpu.CompilerParams(
            collective_id=0, has_side_effects=True, vmem_limit_bytes=67043328
        ),
        name="allegro",
    )(
        features,
        coords,
        migrate_x_slots[0, 0],
        migrate_y_slots[0, 0],
        ghosts,
        neighbours,
        source_weight,
        target_weight,
        radial_weight,
        environ_first,
        mixing_first,
        coupler_first,
        environ_second,
        mixing_second,
        coupler_second,
        readout[None],
    )
    return (forces.reshape(1, 3, 1, count).transpose(0, 2, 1, 3), energies[None])


def solution(mesh):
    in_specs = (
        P("gx", "gy", None, None),
        P("gx", "gy", None, None),
        P("gx", "gy", None, None),
        P("gx", "gy", None, None),
        P("gx", "gy", None),
        P("gx", "gy", None, None),
        P(),
        P(),
        P(),
        P(),
        P(),
        P(),
        P(),
        P(),
        P(),
        P(),
    )
    out_specs = (P("gx", "gy", None, None), P("gx", "gy", None))
    return jax.shard_map(
        functools.partial(per_device, (mesh.shape["gx"], mesh.shape["gy"])),
        mesh=mesh, in_specs=in_specs, out_specs=out_specs, check_vma=False
    )
```

```python
import functools
import math
import types

import jax
import jax.numpy as jnp
from jax import lax
from jax.experimental import pallas as pl
from jax.experimental.pallas import tpu as pltpu
from jax.sharding import PartitionSpec as P

soften = 0.25
cutoff = 2.0
f32 = jnp.float32
bf16 = jnp.bfloat16


def split_two(value):
    top = value.astype(bf16).astype(f32)
    return (top, value - top)


def split_three(value):
    top = value.astype(bf16).astype(f32)
    rest = value - top
    middle = rest.astype(bf16).astype(f32)
    return (top, middle, rest - middle)


def turned(weight):
    return weight.astype(f32).T.astype(bf16)


def product(left, right):
    return jnp.dot(left, right, preferred_element_type=f32)


def product_nt(left, right):
    return lax.dot_general(left, right, (((1,), (1,)), ((), ())), preferred_element_type=f32)


def product_tn(left, right):
    return lax.dot_general(left, right, (((0,), (0,)), ((), ())), preferred_element_type=f32)


def gate_of(half):
    lift = 1.0 + jnp.tanh(half)
    value = half * lift
    return value, lift + value * (2.0 - lift)


def prepare_weights(refs, weights, norm_scale):
    (radial_ref, environ, mixing, coupler, readout_ref) = weights
    breadth = radial_ref.shape[1]
    basis = radial_ref.shape[0]
    w_top, w_low = split_two(radial_ref[...])
    row = readout_ref[...].astype(f32)
    blank = functools.partial(jnp.zeros, dtype=f32)
    left = jnp.concatenate([blank((32, breadth)), w_top, w_low, w_top, blank((8, breadth))], axis=0)
    right = jnp.concatenate(
        [blank((32 + 3 * basis, breadth)), row, row, blank((6, breadth))], axis=0
    )
    refs.first[:, :breadth] = (0.5 * left).astype(bf16)
    refs.first[:, breadth:] = (0.5 * right).astype(bf16)
    last = jnp.concatenate(
        [
            jnp.concatenate([w_top, w_low, blank((16, breadth))], axis=0),
            jnp.concatenate([blank((16, breadth)), row, blank((15, breadth))], axis=0),
        ],
        axis=1,
    )
    refs.last[...] = last.astype(bf16)
    for layer in range(2):
        joined = product(environ[layer][...], coupler[layer][...]) * (0.5 * norm_scale)
        mixed = 0.5 * mixing[layer][...].astype(f32)
        refs.forward[layer, :breadth, :] = mixed.astype(bf16)
        refs.forward[layer, breadth:, :] = joined.astype(bf16)
        refs.backward[layer, :, :breadth] = mixed.T.astype(bf16)
        refs.backward[layer, :, breadth:] = joined.T.astype(bf16)


def prepare_places(refs, place_ref):
    breadth = place_ref.shape[2]
    places = place_ref[...].reshape(-1, breadth)
    refs.split[...] = jnp.concatenate(split_three(places), axis=0).astype(bf16)


def prepare_lists(refs, neighbours):
    slots_per, count = neighbours.shape
    tiles = count // 8
    listed = neighbours[...].astype(f32)
    rows = jnp.concatenate([listed[:, a * tiles : (a + 1) * tiles] for a in range(8)], axis=0)
    refs.listed[...] = rows.T.astype(jnp.int32)


def atom_rows(lanes, slots_per):
    rows = lax.broadcasted_iota(jnp.int32, (16, lanes), 0)
    cols = lax.broadcasted_iota(jnp.int32, (16, lanes), 1)
    return jnp.where(rows == cols // slots_per, 1.0, 0.0)


def chosen(refs, tile, groups, width):
    breadth = refs.listed.shape[1]
    index = jnp.concatenate([refs.listed[pl.ds(tile + u, 1), :] for u in range(width)], axis=1)
    low = index & (breadth - 1)
    high = index >> (breadth.bit_length() - 1)
    rows = lax.broadcasted_iota(jnp.int32, (breadth, width * breadth), 0)
    one_hot = jnp.where(rows == low, 1.0, 0.0).astype(bf16)
    group_rows = lax.broadcasted_iota(jnp.int32, (groups, width * breadth), 0)
    return one_hot, group_rows == high


def geometry(refs, own_ref, basis, slots_per):
    tiles, lanes = refs.listed.shape
    groups = refs.split.shape[0] // 9
    size = 3 * groups
    spread = atom_rows(lanes, slots_per)[:8]
    spread = jnp.concatenate([spread] * 3, axis=0).astype(bf16)
    for k in range(3):
        own = jnp.concatenate(
            [own_ref[k : k + 1, a * tiles : (a + 1) * tiles] for a in range(8)], axis=0
        )
        own = jnp.concatenate(split_three(own), axis=0).astype(bf16)
        refs.dense[3 + k] = product_tn(own, spread)

    @pl.loop(0, tiles // 2, unroll=4)
    def _(pair):
        tile = 2 * pair
        one_hot, in_group = chosen(refs, tile, groups, 2)
        found = product(refs.split[...], one_hot)
        found = found[:size] + found[size : 2 * size] + found[2 * size :]
        for k in range(3):
            far = jnp.sum(
                jnp.where(in_group, found[k * groups : (k + 1) * groups], 0.0),
                axis=0,
                keepdims=True,
            )
            for u in range(2):
                refs.dense[k, pl.ds(tile + u, 1), :] = far[:, u * lanes : (u + 1) * lanes]

    @pl.loop(0, tiles // 8)
    def _(group):
        rows = pl.ds(pl.multiple_of(8 * group, 8), 8)
        offsets = [refs.dense[k, rows, :] - refs.dense[3 + k, rows, :] for k in range(3)]
        square = offsets[0] * offsets[0] + offsets[1] * offsets[1] + offsets[2] * offsets[2]
        length = jnp.sqrt(square + soften)
        inverse = 1.0 / length
        scaled = length / cutoff
        smooth = (1.0 - scaled * scaled) ** 2
        angle = scaled * math.pi
        sine = jnp.sin(angle)
        cosine = jnp.cos(angle)
        factor = inverse * smooth
        for n, value in enumerate(offsets + [length, sine, cosine]):
            refs.dense[n, rows, :] = value
        direction = [offsets[k] * inverse for k in range(3)]
        weighted = [direction[k] * smooth for k in range(3)]
        d_top, d_low = zip(*[split_two(x) for x in direction])
        w_top, w_low = zip(*[split_two(x) for x in weighted])
        before, now = (jnp.zeros_like(sine), sine)
        b_top, b_low = [], []
        for _ in range(basis):
            top, low = split_two(now * factor)
            b_top.append(top)
            b_low.append(low)
            before, now = (now, 2.0 * cosine * now - before)
        s_top, s_low = split_two(smooth)
        blank = jnp.zeros_like(sine)
        left = list(d_top) * 2 + list(d_low) + list(w_top) * 2 + list(w_low) + [blank] * 14
        right = list(w_top) + list(w_low) + list(w_top)
        other = list(d_top) + list(d_low) + list(d_top)
        values = left + b_top + b_top + b_low + [s_top, s_low] + [blank] * 6
        for n, value in enumerate(values):
            start = pl.multiple_of(group * 512 + n * 8, 8)
            refs.narrow[pl.ds(start, 8), :] = value
        for n in range(32):
            start = pl.multiple_of(group * 256 + n * 8, 8)
            refs.pairs[0, pl.ds(start, 8), :] = right[n] if n < 9 else blank
            refs.pairs[1, pl.ds(start, 8), :] = other[n - 9] if 9 <= n < 18 else blank


def spread_tiles(refs):
    tiles = refs.listed.shape[0]

    @pl.loop(0, tiles // 8)
    def _(group):
        for member in range(8):
            tile = group * 8 + member
            whole = refs.narrow[pl.ds(group * 512 + member, 64, stride=8), :].astype(bf16)
            rows = pl.ds(group * 256 + member, 32, stride=8)
            refs.lead[tile] = whole[:32]
            refs.upright[tile] = whole.T
            refs.pair[tile, :, :whole.shape[1]] = refs.pairs[0, rows, :].astype(bf16)
            refs.pair[tile, :, whole.shape[1] :] = refs.pairs[1, rows, :].astype(bf16)


def gather_tile(refs, table_ref, target, at, tile, count, slots_per, rows):
    tiles = count // 8
    for row in rows:
        a, slot = divmod(row, slots_per)
        index = refs.index[slot * count + a * tiles + tile]
        target[pl.ds(at + row, 1), :] = table_ref[pl.ds(index, 1), :]


def sub_block(refs, source_ref, gathered, tile, width, mask, slots_per):
    lanes = gathered.shape[1]
    tiles = source_ref.shape[0] // 8
    size = width * lanes
    upright = [refs.upright[tile + u] for u in range(width)]
    pairs = [refs.pair[tile + u] for u in range(width)]
    stacked = jnp.concatenate(upright, axis=0)
    first = product(stacked, refs.first[...])
    grams = [product(upright[u][:, :32], pairs[u]) for u in range(width)]
    yield
    grams = [(x.astype(bf16) * mask) for x in grams]
    source = jnp.concatenate(
        [
            jnp.broadcast_to(source_ref[pl.ds(a * tiles + tile + u, 1), :], (slots_per, lanes))
            for u in range(width)
            for a in range(8)
        ],
        axis=0,
    )
    half = first[:, :lanes] + source + gathered[...]
    flow = first[:, lanes:]
    value, slope = gate_of(half)
    slopes = [slope]
    hidden = value.astype(bf16)
    kept = [hidden]
    yield
    for layer in range(2):
        around = jnp.concatenate(
            [
                product(grams[u][:, :lanes], hidden[u * lanes : (u + 1) * lanes]).astype(bf16)
                for u in range(width)
            ],
            axis=0,
        )
        yield
        half = product(jnp.concatenate([hidden, around], axis=1), refs.forward[layer])
        yield
        value, slope = gate_of(half)
        hidden = value.astype(bf16)
        slopes.append(slope)
        kept.append(hidden)
        yield
    turns = []
    for layer in (1, 0):
        mixed_grad = (flow * slopes[layer + 1]).astype(bf16)
        back = product(mixed_grad, refs.backward[layer])
        yield
        turn = back[:, lanes:].astype(bf16)
        turns.append(turn)
        flow = back[:, :lanes] + jnp.concatenate(
            [
                product(grams[u][:, lanes:], turn[u * lanes : (u + 1) * lanes])
                for u in range(width)
            ],
            axis=0,
        )
        yield
    paired_grad = (flow * slopes[0]).astype(bf16)
    turns = jnp.concatenate(turns, axis=1)
    inputs = jnp.concatenate([kept[1], kept[0]], axis=1)
    cross = []
    for u in range(width):
        rows = slice(u * lanes, (u + 1) * lanes)
        cross.append(product_nt(turns[rows], inputs[rows]))
    ends = product_nt(refs.last[...], jnp.concatenate([paired_grad, kept[2]], axis=1))
    yield
    cross = [x.astype(bf16) * mask[:, :lanes] for x in cross]
    for u in range(width):
        first_row = pl.multiple_of((tile + u) * 96, 96)
        refs.results[pl.ds(first_row, 32), :] = ends[:, u * lanes : (u + 1) * lanes]
        lead = refs.lead[tile + u]
        refs.results[pl.ds(first_row + 32, 32), :] = product(lead, cross[u])
        refs.results[pl.ds(first_row + 64, 32), :] = product_nt(lead, cross[u])


def main_loop(refs, table_ref, source_ref, slots_per, width, blocks):
    count, lanes = source_ref.shape
    tiles = count // 8
    step = width * blocks
    rows = lax.broadcasted_iota(jnp.int32, (lanes, 2 * lanes), 0) // slots_per
    cols = (lax.broadcasted_iota(jnp.int32, (lanes, 2 * lanes), 1) & (lanes - 1)) // slots_per
    refs.mask[...] = jnp.where(rows == cols, 1.0, 0.0).astype(bf16)

    @pl.loop(0, width * blocks)
    def _(tile):
        for part in range(0, lanes, 16):
            gather_tile(
                refs, table_ref, refs.gathered, tile * lanes, tile, count, slots_per,
                range(part, part + 16),
            )

    @pl.loop(0, tiles // step)
    def _(turn):
        tile = turn * step
        after = jnp.minimum(tile + step, tiles - step)
        mask = refs.mask[...]
        lanes_of = [
            sub_block(
                refs,
                source_ref,
                refs.gathered.at[b * width * lanes : (b + 1) * width * lanes],
                tile + b * width,
                width,
                mask,
                slots_per,
            )
            for b in range(blocks)
        ]
        jobs = []
        for t in range(step):
            for part in range(0, lanes, 32):
                jobs.append((t, range(part, part + 32)))
        live = True
        stage = 0
        while live:
            live = False
            for lane in lanes_of:
                for _ in lane:
                    live = True
                    break
            stage += 1
            if stage >= 2:
                for t, part in jobs[:6]:
                    gather_tile(
                        refs, table_ref, refs.gathered, t * lanes, after + t, count,
                        slots_per, part,
                    )
                jobs = jobs[6:]
        for t, part in jobs:
            gather_tile(
                refs, table_ref, refs.gathered, t * lanes, after + t, count, slots_per, part
            )


def finish(refs, scatter_ref, atom_ref, energy_ref, basis, slots_per):
    tiles, lanes = refs.listed.shape
    groups = scatter_ref.shape[0] // 3
    scatter_ref[...] = jnp.zeros(scatter_ref.shape, f32)

    @pl.loop(0, tiles // 8)
    def _(group):
        rows = pl.ds(pl.multiple_of(8 * group, 8), 8)
        offsets = [refs.dense[k, rows, :] for k in range(3)]
        length, sine, cosine = [refs.dense[3 + k, rows, :] for k in range(3)]
        first = group * (8 * 96)

        def taken(row):
            return refs.results[pl.ds(first + row, 8, stride=96), :]

        inverse = 1.0 / length
        scaled = length / cutoff
        under = 1.0 - scaled * scaled
        smooth = under * under
        direction = [offsets[k] * inverse for k in range(3)]
        sin_before, sin_now = (jnp.zeros_like(sine), sine)
        cos_before, cos_now = (jnp.ones_like(sine), cosine)
        first_sum = jnp.zeros_like(sine)
        second_sum = jnp.zeros_like(sine)
        for b in range(basis):
            grad = taken(b) + taken(basis + b)
            first_sum = first_sum + grad * sin_now
            second_sum = second_sum + grad * (cos_now * ((b + 1) * math.pi / cutoff))
            sin_before, sin_now = (sin_now, 2.0 * cosine * sin_now - sin_before)
            cos_before, cos_now = (cos_now, 2.0 * cosine * cos_now - cos_before)
        edge_energy = taken(16)
        left = [2.0 * (taken(32 + k) + taken(38 + k)) for k in range(3)]
        right = [2.0 * (taken(64 + 9 + k) + taken(64 + 15 + k)) for k in range(3)]
        inner = left[0] * direction[0] + left[1] * direction[1] + left[2] * direction[2]
        turn = [right[k] + smooth * left[k] for k in range(3)]
        smooth_grad = inner + edge_energy + first_sum * inverse
        along = turn[0] * direction[0] + turn[1] * direction[1] + turn[2] * direction[2]
        length_grad = smooth * inverse * (second_sum - first_sum * inverse)
        length_grad = length_grad - smooth_grad * under * (2.0 * scaled / cutoff) * 2.0
        length_grad = length_grad - along * inverse
        for k in range(3):
            refs.dense[k, rows, :] = turn[k] * inverse + length_grad * direction[k]
        refs.dense[3, rows, :] = edge_energy * smooth

    sums = atom_rows(lanes, slots_per).astype(bf16)
    for k in range(4):
        total = jnp.zeros((16, tiles), f32)
        for piece in split_three(refs.dense[k]):
            total = total + product_nt(sums, piece.astype(bf16))
        row = jnp.concatenate([total[a : a + 1] for a in range(8)], axis=1)
        if k == 3:
            energy_ref[...] = row
        else:
            atom_ref[k : k + 1, :] = -row

    @pl.loop(0, tiles // 2, unroll=4)
    def _(pair):
        tile = 2 * pair
        one_hot, in_group = chosen(refs, tile, groups, 2)
        pieces = []
        for k in range(3):
            grad = jnp.concatenate(
                [refs.dense[k, pl.ds(tile + u, 1), :] for u in range(2)], axis=1
            )
            pieces.append(jnp.where(in_group, jnp.broadcast_to(grad, in_group.shape), 0.0))
        spread = jnp.concatenate(pieces, axis=0)
        top = spread.astype(bf16)
        low = (spread - top.astype(f32)).astype(bf16)
        both = product_nt(jnp.concatenate([top, low], axis=0), one_hot)
        scatter_ref[...] += both[: 3 * groups] + both[3 * groups :]


def edge_scratch(count, slots_per, breadth, groups, width, blocks):
    tiles = count // 8
    return dict(
        first=pltpu.VMEM((64, 2 * breadth), bf16),
        last=pltpu.VMEM((32, 2 * breadth), bf16),
        forward=pltpu.VMEM((2, 2 * breadth, breadth), bf16),
        backward=pltpu.VMEM((2, breadth, 2 * breadth), bf16),
        split=pltpu.VMEM((9 * groups, breadth), bf16),
        listed=pltpu.VMEM((tiles, breadth), jnp.int32),
        dense=pltpu.VMEM((6, tiles, breadth), f32),
        narrow=pltpu.VMEM((tiles * 64, breadth), f32),
        pairs=pltpu.VMEM((2, tiles * 32, breadth), f32),
        lead=pltpu.VMEM((tiles, 32, breadth), bf16),
        upright=pltpu.VMEM((tiles, breadth, 64), bf16),
        pair=pltpu.VMEM((tiles, 32, 2 * breadth), bf16),
        gathered=pltpu.VMEM((width * blocks * breadth, breadth), f32),
        results=pltpu.VMEM((tiles * 96, breadth), f32),
        mask=pltpu.VMEM((breadth, 2 * breadth), bf16),
        index=pltpu.SMEM((slots_per * count,), jnp.int32),
    )


def others(shape):
    here = (lax.axis_index("gx"), lax.axis_index("gy"))
    steps = [(n // 3 - 1, n % 3 - 1) for n in range(9)]

    def at(dx, dy):
        return (
            lax.rem(here[0] + (dx + shape[0]), shape[0]),
            lax.rem(here[1] + (dy + shape[1]), shape[1]),
        )

    return (at, steps)


def greet(shape):
    at, steps = others(shape)
    barrier = pltpu.get_barrier_semaphore()
    for dx, dy in steps:
        if (dx, dy) != (0, 0):
            pl.semaphore_signal(
                barrier, inc=1, device_id=at(dx, dy), device_id_type=pl.DeviceIdType.MESH
            )
    return barrier


def send(source, landing, sems, device):
    copy = pltpu.make_async_remote_copy(
        src_ref=source,
        dst_ref=landing,
        send_sem=sems[0],
        recv_sem=sems[1],
        device_id=device,
        device_id_type=pl.DeviceIdType.MESH,
    )
    copy.start()
    return copy


def hot_columns(slots, count):
    rows = lax.broadcasted_iota(jnp.int32, (count, slots.shape[1]), 0)
    return jnp.where(rows == slots, 1.0, 0.0)


def fetch_all(pairs, sems):
    copies = [
        pltpu.make_async_copy(far, near, sems.at[n]) for n, (far, near) in enumerate(pairs)
    ]
    for copy in copies:
        copy.start()
    return copies


def whole_kernel(shape, plan, names, *operands):
    r = types.SimpleNamespace(**dict(zip(names, operands)))
    width, blocks = plan
    slots_per, count = r.neighbours.shape
    breadth = r.features.shape[1]
    sent = r.slots_x.shape[1]
    ghost_count = r.ghosts.shape[1]
    basis = r.radial.shape[0]
    own_groups = count // breadth
    ghost_groups = ghost_count // breadth
    at, steps = others(shape)
    around = [n for n, step in enumerate(steps) if step != (0, 0)]
    barrier = greet(shape)
    fetches = fetch_all(
        [
            (r.features_far, r.features),
            (r.slots_x_far, r.slots_x),
            (r.slots_y_far, r.slots_y),
            (r.ghosts_far, r.ghosts),
            (r.source_weight_far, r.source_weight),
            (r.target_weight_far, r.target_weight),
        ],
        r.fetch_sem,
    )
    lists = fetch_all(
        [
            (r.neighbours.at[slot], r.index.at[pl.ds(slot * count, count)])
            for slot in range(slots_per)
        ],
        r.index_sem,
    )
    later = fetch_all(
        [
            (r.radial_far, r.radial),
            (r.readout_far, r.readout),
            (r.environ_first_far, r.environ_first),
            (r.mixing_first_far, r.mixing_first),
            (r.coupler_first_far, r.coupler_first),
            (r.environ_second_far, r.environ_second),
            (r.mixing_second_far, r.mixing_second),
            (r.coupler_second_far, r.coupler_second),
        ],
        r.later_sem,
    )

    holding = r.holding
    blank = jnp.zeros((5, count), f32)
    pieces = []
    for piece in split_three(r.coords[...].reshape(3, count)):
        pieces += [piece, blank]
    pieces.append(jnp.zeros((breadth - 24, count), f32))
    holding[:, breadth:] = jnp.concatenate(pieces, axis=0).T.astype(bf16)
    for fetch in fetches:
        fetch.wait()
    holding[:, :breadth] = r.features[...]
    moves = [
        jnp.concatenate([n[0:1, :], n[1:2, :]], axis=1) for n in (r.slots_x, r.slots_y)
    ]
    picks = hot_columns(jnp.concatenate(moves, axis=1), count).T.astype(bf16)

    def leave(axis):
        chosen_rows = picks[2 * sent * axis : 2 * sent * (axis + 1)]
        payload = product(chosen_rows, holding[...]).astype(bf16)
        r.leaving[axis, 0] = payload[:sent]
        r.leaving[axis, 1] = payload[sent:]
        if axis == 0:
            pl.semaphore_wait(barrier, 8)
        return [
            send(
                r.leaving.at[axis, way],
                r.arriving.at[axis, way],
                (r.move_send.at[axis, way], r.move_recv.at[axis, way]),
                at(stride, 0) if axis == 0 else at(0, stride),
            )
            for way, stride in ((0, 1), (1, -1))
        ]

    def settle(axis, copies):
        put = hot_columns(moves[axis], count)
        hit = jnp.max(put, axis=1, keepdims=True) > 0.5
        for copy in copies:
            copy.wait()
        came = r.arriving[axis].reshape(2 * sent, 2 * breadth)
        moved = product(put.astype(bf16), came)
        holding[...] = jnp.where(hit, moved, holding[...].astype(f32)).astype(bf16)

    copies = leave(0)
    for fetch in later:
        fetch.wait()
    prepare_weights(
        r,
        (
            r.radial,
            (r.environ_first, r.environ_second),
            (r.mixing_first, r.mixing_second),
            (r.coupler_first, r.coupler_second),
            r.readout,
        ),
        1.0 / math.sqrt(slots_per),
    )
    settle(0, copies)
    copies = leave(1)
    prepare_lists(r, r.neighbours)
    ghost_hot = hot_columns(r.ghosts[...], count)
    ghost_picks = ghost_hot.T.astype(bf16)
    ghost_hot = ghost_hot.astype(bf16)
    settle(1, copies)

    flat = holding[:, breadth:].astype(f32).T[:24]
    ghost_flat = product(flat.astype(bf16), ghost_hot)
    ghost_places = ghost_flat[:8] + ghost_flat[8:16] + ghost_flat[16:24]
    r.ghost_places[...] = ghost_places[:4]
    waits = {}
    for n in around:
        dx, dy = steps[n]
        waits[n] = [
            send(
                r.ghost_places,
                r.halo_places.at[n],
                (r.places_send.at[n], r.places_recv.at[n]),
                at(-dx, -dy),
            )
        ]
    rows = holding[:, :breadth]
    half_target = (0.5 * r.target_weight[...].astype(f32)).astype(bf16)
    half_source = (0.5 * r.source_weight[...].astype(f32)).astype(bf16)
    target = product(rows, half_target).astype(bf16)
    r.ghost_rows[...] = product(ghost_picks, target).astype(bf16)

    def send_rows(source, n, device):
        return send(
            source, r.halo_rows.at[n], (r.rows_send.at[n], r.rows_recv.at[n]), device
        )

    cross = {}
    for n in (1, 7):
        cross[n] = send_rows(r.ghost_rows, n, at(-steps[n][0], 0))
    for n in (3, 5):
        waits[n].append(send_rows(r.ghost_rows, n, at(0, -steps[n][1])))

    r.table[:count, :] = target.astype(f32)
    r.source[...] = product(rows, half_source).astype(bf16).astype(f32)
    mine = flat[:8] + flat[8:16] + flat[16:24]
    r.own[...] = mine
    place = r.place
    place[...] = jnp.zeros(place.shape, f32)
    for k in range(3):
        for g in range(own_groups):
            place[k, g : g + 1, :] = mine[k : k + 1, g * breadth : (g + 1) * breadth]
    rows_at = pl.ds(count + 4 * ghost_count, ghost_count)
    r.table[rows_at, :] = jnp.zeros((ghost_count, breadth), f32)

    r.give[...] = jnp.zeros(r.give.shape, f32)
    for n in (1, 7):
        cross[n].wait()
        for dy in (-1, 1):
            waits[n + dy].append(send_rows(r.halo_rows.at[n], n + dy, at(0, -dy)))
    for n in around:
        waits[n][0].wait()
        places = r.halo_places[n]
        for k in range(3):
            for g in range(ghost_groups):
                group = own_groups + n * ghost_groups + g
                place[k, group : group + 1, :] = places[
                    k : k + 1, g * breadth : (g + 1) * breadth
                ]
    prepare_places(r, place)
    geometry(r, r.own, basis, slots_per)
    spread_tiles(r)
    for copy in lists:
        copy.wait()
    for n in around:
        for copy in waits[n][1:]:
            copy.wait()
        rows_at = pl.ds(count + n * ghost_count, ghost_count)
        r.table[rows_at, :] = r.halo_rows[n].astype(f32)

    main_loop(r, r.table, r.source, slots_per, width, blocks)
    finish(r, r.scatter, r.by_atom, r.energy, basis, slots_per)

    scatter = r.scatter
    groups = scatter.shape[0] // 3
    for n in range(9):
        for g in range(ghost_groups):
            group = own_groups + n * ghost_groups + g
            for k in range(3):
                r.give[n, k : k + 1, g * breadth : (g + 1) * breadth] = scatter[
                    pl.ds(k * groups + group, 1), :
                ]
    copies = {}
    for n in around:
        copies[n] = send(
            r.give.at[n], r.got.at[n], (r.give_send.at[n], r.give_recv.at[n]),
            at(*steps[n]),
        )
    spots = hot_columns(r.ghosts[...], count).T.astype(bf16)
    owns = []
    for k in range(3):
        own = jnp.concatenate(
            [scatter[pl.ds(k * groups + g, 1), :] for g in range(own_groups)], axis=1
        )
        owns.append(own + r.by_atom[k : k + 1, :])
    total = r.give[4][:3]
    for n in around:
        copies[n].wait()
        total = total + r.got[n][:3]
    stack = jnp.concatenate(
        [jnp.concatenate([x, jnp.zeros((5, ghost_count), f32)], axis=0) for x in split_three(total)],
        axis=0,
    ).astype(bf16)
    back = product(stack, spots)
    back = back[:8] + back[8:16] + back[16:24]
    for k in range(3):
        r.force[k] = -(owns[k] + back[k : k + 1, :])


def per_device(
    shape,
    features,
    coords,
    migrate_x_slots,
    migrate_y_slots,
    ghost_slots,
    neighbours,
    source_weight,
    target_weight,
    radial_weight,
    environ_first,
    mixing_first,
    coupler_first,
    environ_second,
    mixing_second,
    coupler_second,
    readout,
):
    features = features[0, 0]
    count, breadth = features.shape
    coords = coords.transpose(0, 2, 1, 3).reshape(3, 1, count)
    neighbours = neighbours[0, 0].T
    ghosts = ghost_slots.reshape(1, -1)
    slots_per = neighbours.shape[0]
    ghost_count = ghosts.shape[1]
    sent = migrate_x_slots.shape[3]
    total_rows = count + 9 * ghost_count
    groups = -(-(total_rows // breadth) // 8) * 8
    width, blocks = 4, 4
    vmem = pl.BlockSpec(memory_space=pltpu.VMEM)
    hbm = pl.BlockSpec(memory_space=pltpu.HBM)
    dma = pltpu.SemaphoreType.DMA
    square = pltpu.VMEM((breadth, breadth), bf16)
    inputs = dict(
        features_far=features,
        coords=coords,
        slots_x_far=migrate_x_slots[0, 0],
        slots_y_far=migrate_y_slots[0, 0],
        ghosts_far=ghosts,
        neighbours=neighbours,
        source_weight_far=source_weight,
        target_weight_far=target_weight,
        radial_far=radial_weight,
        environ_first_far=environ_first,
        mixing_first_far=mixing_first,
        coupler_first_far=coupler_first,
        environ_second_far=environ_second,
        mixing_second_far=mixing_second,
        coupler_second_far=coupler_second,
        readout_far=readout[None],
    )
    scratch = dict(
        features=pltpu.VMEM((count, breadth), bf16),
        slots_x=pltpu.VMEM((2, sent), jnp.int32),
        slots_y=pltpu.VMEM((2, sent), jnp.int32),
        ghosts=pltpu.VMEM((1, ghost_count), jnp.int32),
        source_weight=square,
        target_weight=square,
        radial=pltpu.VMEM(radial_weight.shape, f32),
        readout=pltpu.VMEM((1, breadth), bf16),
        environ_first=square,
        mixing_first=square,
        coupler_first=square,
        environ_second=square,
        mixing_second=square,
        coupler_second=square,
        fetch_sem=dma((6,)),
        index_sem=dma((slots_per,)),
        later_sem=dma((8,)),
        table=pltpu.VMEM((total_rows, breadth), f32),
        source=pltpu.VMEM((count, breadth), f32),
        place=pltpu.VMEM((3, groups, breadth), f32),
        own=pltpu.VMEM((8, count), f32),
        scatter=pltpu.VMEM((3 * groups, breadth), f32),
        by_atom=pltpu.VMEM((8, count), f32),
        holding=pltpu.VMEM((count, 2 * breadth), bf16),
        leaving=pltpu.VMEM((2, 2, sent, 2 * breadth), bf16),
        arriving=pltpu.VMEM((2, 2, sent, 2 * breadth), bf16),
        ghost_rows=pltpu.VMEM((ghost_count, breadth), bf16),
        ghost_places=pltpu.VMEM((4, ghost_count), f32),
        halo_rows=pltpu.VMEM((9, ghost_count, breadth), bf16),
        halo_places=pltpu.VMEM((9, 4, ghost_count), f32),
        give=pltpu.VMEM((9, 4, ghost_count), f32),
        got=pltpu.VMEM((9, 4, ghost_count), f32),
        move_send=dma((2, 2)),
        move_recv=dma((2, 2)),
        rows_send=dma((9,)),
        rows_recv=dma((9,)),
        places_send=dma((9,)),
        places_recv=dma((9,)),
        give_send=dma((9,)),
        give_recv=dma((9,)),
        **edge_scratch(count, slots_per, breadth, groups, width, blocks),
    )
    names = tuple(inputs) + ("force", "energy") + tuple(scratch)
    forces, energies = pl.pallas_call(
        functools.partial(whole_kernel, shape, (width, blocks), names),
        out_shape=(
            jax.ShapeDtypeStruct((3, 1, count), f32),
            jax.ShapeDtypeStruct((1, count), f32),
        ),
        in_specs=[vmem if n in ("coords", "neighbours") else hbm for n in inputs],
        out_specs=(vmem,) * 2,
        scratch_shapes=list(scratch.values()),
        compiler_params=pltpu.CompilerParams(
            collective_id=0, has_side_effects=True, vmem_limit_bytes=67043328
        ),
        name="allegro",
    )(*inputs.values())
    return (forces.reshape(1, 3, 1, count).transpose(0, 2, 1, 3), energies[None])


def solution(mesh):
    in_specs = (
        P("gx", "gy", None, None),
        P("gx", "gy", None, None),
        P("gx", "gy", None, None),
        P("gx", "gy", None, None),
        P("gx", "gy", None),
        P("gx", "gy", None, None),
        P(),
        P(),
        P(),
        P(),
        P(),
        P(),
        P(),
        P(),
        P(),
        P(),
    )
    out_specs = (P("gx", "gy", None, None), P("gx", "gy", None))
    return jax.shard_map(
        functools.partial(per_device, (mesh.shape["gx"], mesh.shape["gy"])),
        mesh=mesh, in_specs=in_specs, out_specs=out_specs, check_vma=False
    )
```

```python
import functools
import math
import types

import jax
import jax.numpy as jnp
from jax import lax
from jax.experimental import pallas as pl
from jax.experimental.pallas import tpu as pltpu
from jax.sharding import PartitionSpec as P

soften = 0.25
cutoff = 2.0
f32 = jnp.float32
bf16 = jnp.bfloat16


def split_two(value):
    top = value.astype(bf16).astype(f32)
    return (top, value - top)


def split_three(value):
    top = value.astype(bf16).astype(f32)
    rest = value - top
    middle = rest.astype(bf16).astype(f32)
    return (top, middle, rest - middle)


def turned(weight):
    return weight.astype(f32).T.astype(bf16)


def product(left, right):
    return jnp.dot(left, right, preferred_element_type=f32)


def product_nt(left, right):
    return lax.dot_general(left, right, (((1,), (1,)), ((), ())), preferred_element_type=f32)


def product_tn(left, right):
    return lax.dot_general(left, right, (((0,), (0,)), ((), ())), preferred_element_type=f32)


def gate_of(half):
    lift = 1.0 + jnp.tanh(half)
    value = half * lift
    return value, lift + value * (2.0 - lift)


def prepare_weights(refs, weights, norm_scale):
    (radial_ref, environ, mixing, coupler, readout_ref) = weights
    breadth = radial_ref.shape[1]
    basis = radial_ref.shape[0]
    w_top, w_low = split_two(radial_ref[...])
    row = readout_ref[...].astype(f32)
    blank = functools.partial(jnp.zeros, dtype=f32)
    left = jnp.concatenate([blank((32, breadth)), w_top, w_low, w_top, blank((8, breadth))], axis=0)
    right = jnp.concatenate(
        [blank((32 + 3 * basis, breadth)), row, row, blank((6, breadth))], axis=0
    )
    refs.first[:, :breadth] = (0.5 * left).astype(bf16)
    refs.first[:, breadth:] = (0.5 * right).astype(bf16)
    last = jnp.concatenate(
        [
            jnp.concatenate([w_top, w_low, blank((16, breadth))], axis=0),
            jnp.concatenate([blank((16, breadth)), row, blank((15, breadth))], axis=0),
        ],
        axis=1,
    )
    refs.last[...] = last.astype(bf16)
    for layer in range(2):
        joined = product(environ[layer][...], coupler[layer][...]) * (0.5 * norm_scale)
        mixed = 0.5 * mixing[layer][...].astype(f32)
        refs.forward[layer, :breadth, :] = mixed.astype(bf16)
        refs.forward[layer, breadth:, :] = joined.astype(bf16)
        refs.backward[layer, :, :breadth] = mixed.T.astype(bf16)
        refs.backward[layer, :, breadth:] = joined.T.astype(bf16)


def prepare_places(refs, place_ref):
    breadth = place_ref.shape[2]
    places = place_ref[...].reshape(-1, breadth)
    refs.split[...] = jnp.concatenate(split_two(places), axis=0).astype(bf16)


def prepare_lists(refs, neighbours):
    slots_per, count = neighbours.shape
    tiles = count // 8
    listed = neighbours[...].astype(f32)
    rows = jnp.concatenate([listed[:, a * tiles : (a + 1) * tiles] for a in range(8)], axis=0)
    refs.listed[...] = rows.T.astype(jnp.int32)


def atom_rows(lanes, slots_per):
    rows = lax.broadcasted_iota(jnp.int32, (16, lanes), 0)
    cols = lax.broadcasted_iota(jnp.int32, (16, lanes), 1)
    return jnp.where(rows == cols // slots_per, 1.0, 0.0)


def index_of(refs, tile, width):
    return jnp.concatenate([refs.listed[pl.ds(tile + u, 1), :] for u in range(width)], axis=1)


def group_of(refs, tile, groups, width):
    breadth = refs.listed.shape[1]
    high = index_of(refs, tile, width) >> (breadth.bit_length() - 1)
    return lax.broadcasted_iota(jnp.int32, (groups, width * breadth), 0) == high


def hot_of(refs, tile, width):
    breadth = refs.listed.shape[1]
    low = index_of(refs, tile, width) & (breadth - 1)
    rows = lax.broadcasted_iota(jnp.int32, (breadth, width * breadth), 0)
    return jnp.where(rows == low, 1.0, 0.0).astype(bf16)


def geometry(refs, own_ref, basis, slots_per):
    tiles, lanes = refs.listed.shape
    groups = refs.split.shape[0] // 6
    size = 3 * groups
    spread = atom_rows(lanes, slots_per)[:8]
    spread = jnp.concatenate([spread] * 3, axis=0).astype(bf16)
    for k in range(3):
        own = jnp.concatenate(
            [own_ref[k : k + 1, a * tiles : (a + 1) * tiles] for a in range(8)], axis=0
        )
        own = jnp.concatenate(split_three(own), axis=0).astype(bf16)
        refs.dense[3 + k] = product_tn(own, spread)

    @pl.loop(0, tiles // 2, unroll=4)
    def _(pair):
        tile = 2 * pair
        one_hot = hot_of(refs, tile, 2)
        in_group = group_of(refs, tile, groups, 2)
        refs.hot[pair] = one_hot
        found = product(refs.split[...], one_hot)
        found = found[:size] + found[size:]
        for k in range(3):
            far = jnp.sum(
                jnp.where(in_group, found[k * groups : (k + 1) * groups], 0.0),
                axis=0,
                keepdims=True,
            )
            for u in range(2):
                refs.dense[k, pl.ds(tile + u, 1), :] = far[:, u * lanes : (u + 1) * lanes]

    @pl.loop(0, tiles // 8)
    def _(group):
        rows = pl.ds(pl.multiple_of(8 * group, 8), 8)
        offsets = [refs.dense[k, rows, :] - refs.dense[3 + k, rows, :] for k in range(3)]
        square = offsets[0] * offsets[0] + offsets[1] * offsets[1] + offsets[2] * offsets[2]
        length = jnp.sqrt(square + soften)
        inverse = 1.0 / length
        scaled = length / cutoff
        smooth = (1.0 - scaled * scaled) ** 2
        angle = scaled * math.pi
        sine = jnp.sin(angle)
        cosine = jnp.cos(angle)
        factor = inverse * smooth
        for n, value in enumerate(offsets + [length, sine, cosine]):
            refs.dense[n, rows, :] = value
        direction = [offsets[k] * inverse for k in range(3)]
        weighted = [direction[k] * smooth for k in range(3)]
        d_top, d_low = zip(*[split_two(x) for x in direction])
        w_top, w_low = zip(*[split_two(x) for x in weighted])
        before, now = (jnp.zeros_like(sine), sine)
        b_top, b_low = [], []
        for _ in range(basis):
            top, low = split_two(now * factor)
            b_top.append(top)
            b_low.append(low)
            before, now = (now, 2.0 * cosine * now - before)
        s_top, s_low = split_two(smooth)
        blank = jnp.zeros_like(sine)
        left = list(d_top) * 2 + list(d_low) + list(w_top) * 2 + list(w_low) + [blank] * 14
        right = list(w_top) + list(w_low) + list(w_top)
        other = list(d_top) + list(d_low) + list(d_top)
        values = left + b_top + b_top + b_low + [s_top, s_low] + [blank] * 6
        for n, value in enumerate(values):
            start = pl.multiple_of(group * 512 + n * 8, 8)
            refs.narrow[pl.ds(start, 8), :] = value
        for n in range(32):
            start = pl.multiple_of(group * 256 + n * 8, 8)
            refs.pairs[0, pl.ds(start, 8), :] = right[n] if n < 9 else blank
            refs.pairs[1, pl.ds(start, 8), :] = other[n - 9] if 9 <= n < 18 else blank


def spread_tiles(refs):
    tiles = refs.listed.shape[0]

    @pl.loop(0, tiles // 8, unroll=2)
    def _(group):
        for member in range(8):
            tile = group * 8 + member
            whole = refs.narrow[pl.ds(group * 512 + member, 64, stride=8), :].astype(bf16)
            rows = pl.ds(group * 256 + member, 32, stride=8)
            refs.lead[tile] = whole[:32]
            refs.upright[tile] = whole.T
            refs.pair[tile, :, :whole.shape[1]] = refs.pairs[0, rows, :].astype(bf16)
            refs.pair[tile, :, whole.shape[1] :] = refs.pairs[1, rows, :].astype(bf16)


def gather_tile(refs, table_ref, target, at, tile, count, slots_per, rows):
    tiles = count // 8
    for row in rows:
        a, slot = divmod(row, slots_per)
        index = refs.index[slot * count + a * tiles + tile]
        target[pl.ds(at + row, 1), :] = table_ref[pl.ds(index, 1), :]


def sub_block(refs, source_ref, gathered, tile, width, mask, slots_per):
    lanes = gathered.shape[1]
    tiles = source_ref.shape[0] // 8
    size = width * lanes
    upright = [refs.upright[tile + u] for u in range(width)]
    pairs = [refs.pair[tile + u] for u in range(width)]
    stacked = jnp.concatenate(upright, axis=0)
    first = product(stacked, refs.first[...])
    grams = [product(upright[u][:, :32], pairs[u]) for u in range(width)]
    yield
    grams = [(x.astype(bf16) * mask) for x in grams]
    source = jnp.concatenate(
        [
            jnp.broadcast_to(source_ref[pl.ds(a * tiles + tile + u, 1), :], (slots_per, lanes))
            for u in range(width)
            for a in range(8)
        ],
        axis=0,
    )
    half = first[:, :lanes] + source + gathered[...]
    flow = first[:, lanes:]
    value, slope = gate_of(half)
    slopes = [slope]
    hidden = value.astype(bf16)
    kept = [hidden]
    yield
    for layer in range(2):
        around = jnp.concatenate(
            [
                product(grams[u][:, :lanes], hidden[u * lanes : (u + 1) * lanes]).astype(bf16)
                for u in range(width)
            ],
            axis=0,
        )
        yield
        half = product(jnp.concatenate([hidden, around], axis=1), refs.forward[layer])
        yield
        value, slope = gate_of(half)
        hidden = value.astype(bf16)
        slopes.append(slope)
        kept.append(hidden)
        yield
    turns = []
    for layer in (1, 0):
        mixed_grad = (flow * slopes[layer + 1]).astype(bf16)
        back = product(mixed_grad, refs.backward[layer])
        yield
        turn = back[:, lanes:].astype(bf16)
        turns.append(turn)
        flow = back[:, :lanes] + jnp.concatenate(
            [
                product(grams[u][:, lanes:], turn[u * lanes : (u + 1) * lanes])
                for u in range(width)
            ],
            axis=0,
        )
        yield
    paired_grad = (flow * slopes[0]).astype(bf16)
    turns = jnp.concatenate(turns, axis=1)
    inputs = jnp.concatenate([kept[1], kept[0]], axis=1)
    cross = []
    for u in range(width):
        rows = slice(u * lanes, (u + 1) * lanes)
        cross.append(product_nt(turns[rows], inputs[rows]))
    ends = product_nt(refs.last[...], jnp.concatenate([paired_grad, kept[2]], axis=1))
    yield
    cross = [x.astype(bf16) * mask[:, :lanes] for x in cross]
    for u in range(width):
        first_row = pl.multiple_of((tile + u) * 96, 96)
        refs.results[pl.ds(first_row, 32), :] = ends[:, u * lanes : (u + 1) * lanes]
        lead = refs.lead[tile + u]
        refs.results[pl.ds(first_row + 32, 32), :] = product(lead, cross[u])
        refs.results[pl.ds(first_row + 64, 32), :] = product_nt(lead, cross[u])


def main_loop(refs, table_ref, source_ref, slots_per, width, blocks):
    count, lanes = source_ref.shape
    tiles = count // 8
    step = width * blocks
    rows = lax.broadcasted_iota(jnp.int32, (lanes, 2 * lanes), 0) // slots_per
    cols = (lax.broadcasted_iota(jnp.int32, (lanes, 2 * lanes), 1) & (lanes - 1)) // slots_per
    refs.mask[...] = jnp.where(rows == cols, 1.0, 0.0).astype(bf16)

    for tile in range(step):
        gather_tile(
            refs, table_ref, refs.gathered, tile * lanes, tile, count, slots_per, range(lanes)
        )

    @pl.loop(0, tiles // step)
    def _(turn):
        tile = turn * step
        after = jnp.minimum(tile + step, tiles - step)
        mask = refs.mask[...]
        lanes_of = [
            sub_block(
                refs,
                source_ref,
                refs.gathered.at[b * width * lanes : (b + 1) * width * lanes],
                tile + b * width,
                width,
                mask,
                slots_per,
            )
            for b in range(blocks)
        ]
        jobs = []
        for t in range(step):
            for part in range(0, lanes, 32):
                jobs.append((t, range(part, part + 32)))
        live = True
        stage = 0
        while live:
            live = False
            for lane in lanes_of:
                for _ in lane:
                    live = True
                    break
            stage += 1
            if stage >= 2:
                for t, part in jobs[:6]:
                    gather_tile(
                        refs, table_ref, refs.gathered, t * lanes, after + t, count,
                        slots_per, part,
                    )
                jobs = jobs[6:]
        for t, part in jobs:
            gather_tile(
                refs, table_ref, refs.gathered, t * lanes, after + t, count, slots_per, part
            )


def finish(refs, scatter_ref, basis):
    tiles, lanes = refs.listed.shape
    groups = scatter_ref.shape[0] // 3
    scatter_ref[...] = jnp.zeros(scatter_ref.shape, f32)

    @pl.loop(0, tiles // 8)
    def _(group):
        rows = pl.ds(pl.multiple_of(8 * group, 8), 8)
        offsets = [refs.dense[k, rows, :] for k in range(3)]
        length, sine, cosine = [refs.dense[3 + k, rows, :] for k in range(3)]
        first = group * (8 * 96)

        def taken(row):
            return refs.results[pl.ds(first + row, 8, stride=96), :]

        inverse = 1.0 / length
        scaled = length / cutoff
        under = 1.0 - scaled * scaled
        smooth = under * under
        direction = [offsets[k] * inverse for k in range(3)]
        sin_before, sin_now = (jnp.zeros_like(sine), sine)
        cos_before, cos_now = (jnp.ones_like(sine), cosine)
        first_sum = jnp.zeros_like(sine)
        second_sum = jnp.zeros_like(sine)
        for b in range(basis):
            grad = taken(b) + taken(basis + b)
            first_sum = first_sum + grad * sin_now
            second_sum = second_sum + grad * (cos_now * ((b + 1) * math.pi / cutoff))
            sin_before, sin_now = (sin_now, 2.0 * cosine * sin_now - sin_before)
            cos_before, cos_now = (cos_now, 2.0 * cosine * cos_now - cos_before)
        edge_energy = taken(16)
        left = [2.0 * (taken(32 + k) + taken(38 + k)) for k in range(3)]
        right = [2.0 * (taken(64 + 9 + k) + taken(64 + 15 + k)) for k in range(3)]
        inner = left[0] * direction[0] + left[1] * direction[1] + left[2] * direction[2]
        turn = [right[k] + smooth * left[k] for k in range(3)]
        smooth_grad = inner + edge_energy + first_sum * inverse
        along = turn[0] * direction[0] + turn[1] * direction[1] + turn[2] * direction[2]
        length_grad = smooth * inverse * (second_sum - first_sum * inverse)
        length_grad = length_grad - smooth_grad * under * (2.0 * scaled / cutoff) * 2.0
        length_grad = length_grad - along * inverse
        for k in range(3):
            refs.dense[k, rows, :] = turn[k] * inverse + length_grad * direction[k]
        refs.dense[3, rows, :] = edge_energy * smooth

    @pl.loop(0, tiles // 2, unroll=4)
    def _(pair):
        tile = 2 * pair
        in_group = group_of(refs, tile, groups, 2)
        pieces = []
        for k in range(3):
            grad = jnp.concatenate(
                [refs.dense[k, pl.ds(tile + u, 1), :] for u in range(2)], axis=1
            )
            pieces.append(jnp.where(in_group, jnp.broadcast_to(grad, in_group.shape), 0.0))
        spread = jnp.concatenate(pieces, axis=0)
        scatter_ref[...] += product_nt(spread.astype(bf16), refs.hot[pair])


def gather_atoms(refs, atom_ref, energy_ref, slots_per):
    tiles, lanes = refs.listed.shape
    sums = atom_rows(lanes, slots_per).astype(bf16)
    for k in range(4):
        total = jnp.zeros((16, tiles), f32)
        for piece in split_three(refs.dense[k]):
            total = total + product_nt(sums, piece.astype(bf16))
        row = jnp.concatenate([total[a : a + 1] for a in range(8)], axis=1)
        if k == 3:
            energy_ref[...] = row
        else:
            atom_ref[k : k + 1, :] = -row


def edge_scratch(count, slots_per, breadth, groups, width, blocks):
    tiles = count // 8
    return dict(
        first=pltpu.VMEM((64, 2 * breadth), bf16),
        last=pltpu.VMEM((32, 2 * breadth), bf16),
        forward=pltpu.VMEM((2, 2 * breadth, breadth), bf16),
        backward=pltpu.VMEM((2, breadth, 2 * breadth), bf16),
        split=pltpu.VMEM((6 * groups, breadth), bf16),
        listed=pltpu.VMEM((tiles, breadth), jnp.int32),
        dense=pltpu.VMEM((6, tiles, breadth), f32),
        narrow=pltpu.VMEM((tiles * 64, breadth), f32),
        pairs=pltpu.VMEM((2, tiles * 32, breadth), f32),
        lead=pltpu.VMEM((tiles, 32, breadth), bf16),
        upright=pltpu.VMEM((tiles, breadth, 64), bf16),
        pair=pltpu.VMEM((tiles, 32, 2 * breadth), bf16),
        gathered=pltpu.VMEM((width * blocks * breadth, breadth), f32),
        results=pltpu.VMEM((tiles * 96, breadth), f32),
        hot=pltpu.VMEM((tiles // 2, breadth, 2 * breadth), bf16),
        mask=pltpu.VMEM((breadth, 2 * breadth), bf16),
        index=pltpu.SMEM((slots_per * count,), jnp.int32),
    )


def others(shape):
    here = (lax.axis_index("gx"), lax.axis_index("gy"))
    steps = [(n // 3 - 1, n % 3 - 1) for n in range(9)]

    def at(dx, dy):
        return (
            lax.rem(here[0] + (dx + shape[0]), shape[0]),
            lax.rem(here[1] + (dy + shape[1]), shape[1]),
        )

    return (at, steps)


def greet(shape):
    at, steps = others(shape)
    barrier = pltpu.get_barrier_semaphore()
    for dx, dy in steps:
        if (dx, dy) != (0, 0):
            pl.semaphore_signal(
                barrier, inc=1, device_id=at(dx, dy), device_id_type=pl.DeviceIdType.MESH
            )
    return barrier


def send(source, landing, sems, device):
    copy = pltpu.make_async_remote_copy(
        src_ref=source,
        dst_ref=landing,
        send_sem=sems[0],
        recv_sem=sems[1],
        device_id=device,
        device_id_type=pl.DeviceIdType.MESH,
    )
    copy.start()
    return copy


def hot_columns(slots, count):
    rows = lax.broadcasted_iota(jnp.int32, (count, slots.shape[1]), 0)
    return jnp.where(rows == slots, 1.0, 0.0)


def fetch_all(pairs, sems):
    copies = [
        pltpu.make_async_copy(far, near, sems.at[n]) for n, (far, near) in enumerate(pairs)
    ]
    for copy in copies:
        copy.start()
    return copies


def whole_kernel(shape, plan, names, *operands):
    r = types.SimpleNamespace(**dict(zip(names, operands)))
    width, blocks = plan
    slots_per, count = r.neighbours.shape
    breadth = r.features.shape[1]
    sent = r.slots_x.shape[1]
    ghost_count = r.ghosts.shape[1]
    basis = r.radial.shape[0]
    own_groups = count // breadth
    ghost_groups = ghost_count // breadth
    at, steps = others(shape)
    around = [n for n, step in enumerate(steps) if step != (0, 0)]
    barrier = greet(shape)
    fetches = fetch_all(
        [
            (r.features_far, r.features),
            (r.slots_x_far, r.slots_x),
            (r.slots_y_far, r.slots_y),
            (r.ghosts_far, r.ghosts),
            (r.source_weight_far, r.source_weight),
            (r.target_weight_far, r.target_weight),
        ],
        r.fetch_sem,
    )
    lists = fetch_all(
        [
            (r.neighbours.at[slot], r.index.at[pl.ds(slot * count, count)])
            for slot in range(slots_per)
        ],
        r.index_sem,
    )
    later = fetch_all(
        [
            (r.radial_far, r.radial),
            (r.readout_far, r.readout),
            (r.environ_first_far, r.environ_first),
            (r.mixing_first_far, r.mixing_first),
            (r.coupler_first_far, r.coupler_first),
            (r.environ_second_far, r.environ_second),
            (r.mixing_second_far, r.mixing_second),
            (r.coupler_second_far, r.coupler_second),
        ],
        r.later_sem,
    )

    holding = r.holding
    blank = jnp.zeros((5, count), f32)
    pieces = []
    for piece in split_three(r.coords[...].reshape(3, count)):
        pieces += [piece, blank]
    pieces.append(jnp.zeros((breadth - 24, count), f32))
    holding[:, breadth:] = jnp.concatenate(pieces, axis=0).T.astype(bf16)
    for fetch in fetches:
        fetch.wait()
    holding[:, :breadth] = r.features[...]
    moves = [
        jnp.concatenate([n[0:1, :], n[1:2, :]], axis=1) for n in (r.slots_x, r.slots_y)
    ]
    picks = hot_columns(jnp.concatenate(moves, axis=1), count).T.astype(bf16)

    def leave(axis):
        chosen_rows = picks[2 * sent * axis : 2 * sent * (axis + 1)]
        payload = product(chosen_rows, holding[...]).astype(bf16)
        r.leaving[axis, 0] = payload[:sent]
        r.leaving[axis, 1] = payload[sent:]
        if axis == 0:
            pl.semaphore_wait(barrier, 8)
        return [
            send(
                r.leaving.at[axis, way],
                r.arriving.at[axis, way],
                (r.move_send.at[axis, way], r.move_recv.at[axis, way]),
                at(stride, 0) if axis == 0 else at(0, stride),
            )
            for way, stride in ((0, 1), (1, -1))
        ]

    def settle(axis, copies):
        put = hot_columns(moves[axis], count)
        hit = jnp.max(put, axis=1, keepdims=True) > 0.5
        for copy in copies:
            copy.wait()
        came = r.arriving[axis].reshape(2 * sent, 2 * breadth)
        moved = product(put.astype(bf16), came)
        holding[...] = jnp.where(hit, moved, holding[...].astype(f32)).astype(bf16)

    copies = leave(0)
    for fetch in later:
        fetch.wait()
    prepare_weights(
        r,
        (
            r.radial,
            (r.environ_first, r.environ_second),
            (r.mixing_first, r.mixing_second),
            (r.coupler_first, r.coupler_second),
            r.readout,
        ),
        1.0 / math.sqrt(slots_per),
    )
    settle(0, copies)
    copies = leave(1)
    prepare_lists(r, r.neighbours)
    ghost_hot = hot_columns(r.ghosts[...], count)
    ghost_picks = ghost_hot.T.astype(bf16)
    ghost_hot = ghost_hot.astype(bf16)
    settle(1, copies)

    flat = holding[:, breadth:].astype(f32).T[:24]
    ghost_flat = product(flat.astype(bf16), ghost_hot)
    ghost_places = ghost_flat[:8] + ghost_flat[8:16] + ghost_flat[16:24]
    r.ghost_places[...] = ghost_places[:4]
    waits = {}
    for n in around:
        dx, dy = steps[n]
        waits[n] = [
            send(
                r.ghost_places,
                r.halo_places.at[n],
                (r.places_send.at[n], r.places_recv.at[n]),
                at(-dx, -dy),
            )
        ]
    rows = holding[:, :breadth]
    half_target = (0.5 * r.target_weight[...].astype(f32)).astype(bf16)
    half_source = (0.5 * r.source_weight[...].astype(f32)).astype(bf16)
    target = product(rows, half_target).astype(bf16)
    chunks = [pl.ds(c * (ghost_count // 2), ghost_count // 2) for c in range(2)]

    def send_rows(source, n, c, device):
        return send(
            source.at[chunks[c]],
            r.halo_rows.at[n, chunks[c]],
            (r.rows_send.at[n, c], r.rows_recv.at[n, c]),
            device,
        )

    cross = {}
    for c in range(2):
        part = slice(c * (ghost_count // 2), (c + 1) * (ghost_count // 2))
        r.ghost_rows[part] = product(ghost_picks[part], target).astype(bf16)
        for n in (1, 7):
            cross[n, c] = send_rows(r.ghost_rows, n, c, at(-steps[n][0], 0))
    for c in range(2):
        for n in (3, 5):
            waits[n].append(send_rows(r.ghost_rows, n, c, at(0, -steps[n][1])))

    r.table[:count, :] = target.astype(f32)
    r.source[...] = product(rows, half_source).astype(bf16).astype(f32)
    mine = flat[:8] + flat[8:16] + flat[16:24]
    r.own[...] = mine
    place = r.place
    place[...] = jnp.zeros(place.shape, f32)
    for k in range(3):
        for g in range(own_groups):
            place[k, g : g + 1, :] = mine[k : k + 1, g * breadth : (g + 1) * breadth]
    rows_at = pl.ds(count + 4 * ghost_count, ghost_count)
    r.table[rows_at, :] = jnp.zeros((ghost_count, breadth), f32)

    r.give[...] = jnp.zeros(r.give.shape, f32)
    for c in range(2):
        for n in (1, 7):
            cross[n, c].wait()
            for dy in (-1, 1):
                waits[n + dy].append(send_rows(r.halo_rows.at[n], n + dy, c, at(0, -dy)))
    for n in around:
        waits[n][0].wait()
        places = r.halo_places[n]
        for k in range(3):
            for g in range(ghost_groups):
                group = own_groups + n * ghost_groups + g
                place[k, group : group + 1, :] = places[
                    k : k + 1, g * breadth : (g + 1) * breadth
                ]
    prepare_places(r, place)
    geometry(r, r.own, basis, slots_per)
    spread_tiles(r)
    for copy in lists:
        copy.wait()
    for n in around:
        for copy in waits[n][1:]:
            copy.wait()
        rows_at = pl.ds(count + n * ghost_count, ghost_count)
        r.table[rows_at, :] = r.halo_rows[n].astype(f32)

    main_loop(r, r.table, r.source, slots_per, width, blocks)
    finish(r, r.scatter, basis)

    scatter = r.scatter
    groups = scatter.shape[0] // 3
    for n in range(9):
        for g in range(ghost_groups):
            group = own_groups + n * ghost_groups + g
            for k in range(3):
                r.give[n, k : k + 1, g * breadth : (g + 1) * breadth] = scatter[
                    pl.ds(k * groups + group, 1), :
                ]
    copies = {}
    for n in around:
        copies[n] = send(
            r.give.at[n], r.got.at[n], (r.give_send.at[n], r.give_recv.at[n]),
            at(*steps[n]),
        )
    gather_atoms(r, r.by_atom, r.energy, slots_per)
    spots = hot_columns(r.ghosts[...], count).T.astype(bf16)
    owns = []
    for k in range(3):
        own = jnp.concatenate(
            [scatter[pl.ds(k * groups + g, 1), :] for g in range(own_groups)], axis=1
        )
        owns.append(own + r.by_atom[k : k + 1, :])
    total = r.give[4][:3]
    for n in around:
        copies[n].wait()
        total = total + r.got[n][:3]
    stack = jnp.concatenate(
        [jnp.concatenate([x, jnp.zeros((5, ghost_count), f32)], axis=0) for x in split_three(total)],
        axis=0,
    ).astype(bf16)
    back = product(stack, spots)
    back = back[:8] + back[8:16] + back[16:24]
    for k in range(3):
        r.force[k] = -(owns[k] + back[k : k + 1, :])


def per_device(
    shape,
    features,
    coords,
    migrate_x_slots,
    migrate_y_slots,
    ghost_slots,
    neighbours,
    source_weight,
    target_weight,
    radial_weight,
    environ_first,
    mixing_first,
    coupler_first,
    environ_second,
    mixing_second,
    coupler_second,
    readout,
):
    features = features[0, 0]
    count, breadth = features.shape
    coords = coords.transpose(0, 2, 1, 3).reshape(3, 1, count)
    neighbours = neighbours[0, 0].T
    ghosts = ghost_slots.reshape(1, -1)
    slots_per = neighbours.shape[0]
    ghost_count = ghosts.shape[1]
    sent = migrate_x_slots.shape[3]
    total_rows = count + 9 * ghost_count
    groups = -(-(total_rows // breadth) // 8) * 8
    width, blocks = 4, 4
    vmem = pl.BlockSpec(memory_space=pltpu.VMEM)
    hbm = pl.BlockSpec(memory_space=pltpu.HBM)
    dma = pltpu.SemaphoreType.DMA
    square = pltpu.VMEM((breadth, breadth), bf16)
    inputs = dict(
        features_far=features,
        coords=coords,
        slots_x_far=migrate_x_slots[0, 0],
        slots_y_far=migrate_y_slots[0, 0],
        ghosts_far=ghosts,
        neighbours=neighbours,
        source_weight_far=source_weight,
        target_weight_far=target_weight,
        radial_far=radial_weight,
        environ_first_far=environ_first,
        mixing_first_far=mixing_first,
        coupler_first_far=coupler_first,
        environ_second_far=environ_second,
        mixing_second_far=mixing_second,
        coupler_second_far=coupler_second,
        readout_far=readout[None],
    )
    scratch = dict(
        features=pltpu.VMEM((count, breadth), bf16),
        slots_x=pltpu.VMEM((2, sent), jnp.int32),
        slots_y=pltpu.VMEM((2, sent), jnp.int32),
        ghosts=pltpu.VMEM((1, ghost_count), jnp.int32),
        source_weight=square,
        target_weight=square,
        radial=pltpu.VMEM(radial_weight.shape, f32),
        readout=pltpu.VMEM((1, breadth), bf16),
        environ_first=square,
        mixing_first=square,
        coupler_first=square,
        environ_second=square,
        mixing_second=square,
        coupler_second=square,
        fetch_sem=dma((6,)),
        index_sem=dma((slots_per,)),
        later_sem=dma((8,)),
        table=pltpu.VMEM((total_rows, breadth), f32),
        source=pltpu.VMEM((count, breadth), f32),
        place=pltpu.VMEM((3, groups, breadth), f32),
        own=pltpu.VMEM((8, count), f32),
        scatter=pltpu.VMEM((3 * groups, breadth), f32),
        by_atom=pltpu.VMEM((8, count), f32),
        holding=pltpu.VMEM((count, 2 * breadth), bf16),
        leaving=pltpu.VMEM((2, 2, sent, 2 * breadth), bf16),
        arriving=pltpu.VMEM((2, 2, sent, 2 * breadth), bf16),
        ghost_rows=pltpu.VMEM((ghost_count, breadth), bf16),
        ghost_places=pltpu.VMEM((4, ghost_count), f32),
        halo_rows=pltpu.VMEM((9, ghost_count, breadth), bf16),
        halo_places=pltpu.VMEM((9, 4, ghost_count), f32),
        give=pltpu.VMEM((9, 4, ghost_count), f32),
        got=pltpu.VMEM((9, 4, ghost_count), f32),
        move_send=dma((2, 2)),
        move_recv=dma((2, 2)),
        rows_send=dma((9, 2)),
        rows_recv=dma((9, 2)),
        places_send=dma((9,)),
        places_recv=dma((9,)),
        give_send=dma((9,)),
        give_recv=dma((9,)),
        **edge_scratch(count, slots_per, breadth, groups, width, blocks),
    )
    names = tuple(inputs) + ("force", "energy") + tuple(scratch)
    forces, energies = pl.pallas_call(
        functools.partial(whole_kernel, shape, (width, blocks), names),
        out_shape=(
            jax.ShapeDtypeStruct((3, 1, count), f32),
            jax.ShapeDtypeStruct((1, count), f32),
        ),
        in_specs=[vmem if n in ("coords", "neighbours") else hbm for n in inputs],
        out_specs=(vmem,) * 2,
        scratch_shapes=list(scratch.values()),
        compiler_params=pltpu.CompilerParams(
            collective_id=0, has_side_effects=True, vmem_limit_bytes=67043328
        ),
        name="allegro",
    )(*inputs.values())
    return (forces.reshape(1, 3, 1, count).transpose(0, 2, 1, 3), energies[None])


def solution(mesh):
    in_specs = (
        P("gx", "gy", None, None),
        P("gx", "gy", None, None),
        P("gx", "gy", None, None),
        P("gx", "gy", None, None),
        P("gx", "gy", None),
        P("gx", "gy", None, None),
        P(),
        P(),
        P(),
        P(),
        P(),
        P(),
        P(),
        P(),
        P(),
        P(),
    )
    out_specs = (P("gx", "gy", None, None), P("gx", "gy", None))
    return jax.shard_map(
        functools.partial(per_device, (mesh.shape["gx"], mesh.shape["gy"])),
        mesh=mesh, in_specs=in_specs, out_specs=out_specs, check_vma=False
    )
```

```python
import functools
import math
import types

import jax
import jax.numpy as jnp
from jax import lax
from jax.experimental import pallas as pl
from jax.experimental.pallas import tpu as pltpu
from jax.sharding import PartitionSpec as P

soften = 0.25
cutoff = 2.0
f32 = jnp.float32
bf16 = jnp.bfloat16


def split_two(value):
    top = value.astype(bf16).astype(f32)
    return (top, value - top)


def split_three(value):
    top = value.astype(bf16).astype(f32)
    rest = value - top
    middle = rest.astype(bf16).astype(f32)
    return (top, middle, rest - middle)


def turned(weight):
    return weight.astype(f32).T.astype(bf16)


def product(left, right):
    return jnp.dot(left, right, preferred_element_type=f32)


def product_nt(left, right):
    return lax.dot_general(left, right, (((1,), (1,)), ((), ())), preferred_element_type=f32)


def product_tn(left, right):
    return lax.dot_general(left, right, (((0,), (0,)), ((), ())), preferred_element_type=f32)


def gate_of(half):
    lift = 1.0 + jnp.tanh(half)
    value = half * lift
    return value, lift + value * (2.0 - lift)


def prepare_weights(refs, weights, norm_scale):
    (radial_ref, environ, mixing, coupler, readout_ref) = weights
    breadth = radial_ref.shape[1]
    basis = radial_ref.shape[0]
    w_top, w_low = split_two(radial_ref[...])
    row = readout_ref[...].astype(f32)
    blank = functools.partial(jnp.zeros, dtype=f32)
    left = jnp.concatenate([blank((32, breadth)), w_top, w_low, w_top, blank((8, breadth))], axis=0)
    right = jnp.concatenate(
        [blank((32 + 3 * basis, breadth)), row, row, blank((6, breadth))], axis=0
    )
    refs.first[:, :breadth] = (0.5 * left).astype(bf16)
    refs.first[:, breadth:] = (0.5 * right).astype(bf16)
    last = jnp.concatenate(
        [
            jnp.concatenate([w_top, w_low, blank((16, breadth))], axis=0),
            jnp.concatenate([blank((16, breadth)), row, blank((15, breadth))], axis=0),
        ],
        axis=1,
    )
    refs.last[...] = last.astype(bf16)
    for layer in range(2):
        joined = product(environ[layer][...], coupler[layer][...]) * (0.5 * norm_scale)
        mixed = 0.5 * mixing[layer][...].astype(f32)
        refs.forward[layer, :breadth, :] = mixed.astype(bf16)
        refs.forward[layer, breadth:, :] = joined.astype(bf16)
        refs.backward[layer, :, :breadth] = mixed.T.astype(bf16)
        refs.backward[layer, :, breadth:] = joined.T.astype(bf16)


def prepare_places(refs, place_ref):
    breadth = place_ref.shape[2]
    places = place_ref[...].reshape(-1, breadth)
    refs.split[...] = jnp.concatenate(split_two(places), axis=0).astype(bf16)


def prepare_lists(refs, neighbours):
    slots_per, count = neighbours.shape
    tiles = count // 8
    listed = neighbours[...].astype(f32)
    rows = jnp.concatenate([listed[:, a * tiles : (a + 1) * tiles] for a in range(8)], axis=0)
    refs.listed[...] = rows.T.astype(jnp.int32)


def atom_rows(lanes, slots_per):
    rows = lax.broadcasted_iota(jnp.int32, (16, lanes), 0)
    cols = lax.broadcasted_iota(jnp.int32, (16, lanes), 1)
    return jnp.where(rows == cols // slots_per, 1.0, 0.0)


def index_of(refs, tile, width):
    return jnp.concatenate([refs.listed[pl.ds(tile + u, 1), :] for u in range(width)], axis=1)


def group_of(refs, tile, groups, width):
    breadth = refs.listed.shape[1]
    high = index_of(refs, tile, width) >> (breadth.bit_length() - 1)
    return lax.broadcasted_iota(jnp.int32, (groups, width * breadth), 0) == high


def hot_of(refs, tile, width):
    breadth = refs.listed.shape[1]
    low = index_of(refs, tile, width) & (breadth - 1)
    rows = lax.broadcasted_iota(jnp.int32, (breadth, width * breadth), 0)
    return jnp.where(rows == low, 1.0, 0.0).astype(bf16)


def geometry(refs, own_ref, basis, slots_per):
    tiles, lanes = refs.listed.shape
    groups = refs.split.shape[0] // 6
    size = 3 * groups
    spread = atom_rows(lanes, slots_per)[:8]
    spread = jnp.concatenate([spread] * 3, axis=0).astype(bf16)
    for k in range(3):
        own = jnp.concatenate(
            [own_ref[k : k + 1, a * tiles : (a + 1) * tiles] for a in range(8)], axis=0
        )
        own = jnp.concatenate(split_three(own), axis=0).astype(bf16)
        refs.dense[3 + k] = product_tn(own, spread)

    @pl.loop(0, tiles // 2, unroll=4)
    def _(pair):
        tile = 2 * pair
        one_hot = hot_of(refs, tile, 2)
        in_group = group_of(refs, tile, groups, 2)
        refs.hot[pair] = one_hot
        found = product(refs.split[...], one_hot)
        found = found[:size] + found[size:]
        for k in range(3):
            far = jnp.sum(
                jnp.where(in_group, found[k * groups : (k + 1) * groups], 0.0),
                axis=0,
                keepdims=True,
            )
            for u in range(2):
                refs.dense[k, pl.ds(tile + u, 1), :] = far[:, u * lanes : (u + 1) * lanes]

    @pl.loop(0, tiles // 8, unroll=2)
    def _(group):
        rows = pl.ds(pl.multiple_of(8 * group, 8), 8)
        offsets = [refs.dense[k, rows, :] - refs.dense[3 + k, rows, :] for k in range(3)]
        square = offsets[0] * offsets[0] + offsets[1] * offsets[1] + offsets[2] * offsets[2]
        length = jnp.sqrt(square + soften)
        inverse = 1.0 / length
        scaled = length / cutoff
        smooth = (1.0 - scaled * scaled) ** 2
        angle = scaled * math.pi
        sine = jnp.sin(angle)
        cosine = jnp.cos(angle)
        factor = inverse * smooth
        for n, value in enumerate(offsets + [length, sine, cosine]):
            refs.dense[n, rows, :] = value
        direction = [offsets[k] * inverse for k in range(3)]
        weighted = [direction[k] * smooth for k in range(3)]
        d_top, d_low = zip(*[split_two(x) for x in direction])
        w_top, w_low = zip(*[split_two(x) for x in weighted])
        before, now = (jnp.zeros_like(sine), sine)
        b_top, b_low = [], []
        for _ in range(basis):
            top, low = split_two(now * factor)
            b_top.append(top)
            b_low.append(low)
            before, now = (now, 2.0 * cosine * now - before)
        s_top, s_low = split_two(smooth)
        blank = jnp.zeros_like(sine)
        left = list(d_top) * 2 + list(d_low) + list(w_top) * 2 + list(w_low) + [blank] * 14
        right = list(w_top) + list(w_low) + list(w_top)
        values = left + b_top + b_top + b_low + [s_top, s_low] + [blank] * 6
        for n, value in enumerate(values):
            start = pl.multiple_of(group * 512 + n * 8, 8)
            refs.narrow[pl.ds(start, 8), :] = value
        for n in range(16):
            start = pl.multiple_of(group * 128 + n * 8, 8)
            refs.pairs[pl.ds(start, 8), :] = right[n] if n < 9 else blank


def spread_tiles(refs):
    tiles = refs.listed.shape[0]

    @pl.loop(0, tiles // 8, unroll=2)
    def _(group):
        for member in range(8):
            tile = group * 8 + member
            whole = refs.narrow[pl.ds(group * 512 + member, 64, stride=8), :].astype(bf16)
            rows = pl.ds(group * 128 + member, 16, stride=8)
            refs.lead[tile] = whole[:32]
            refs.upright[tile] = whole.T
            refs.pair[tile] = refs.pairs[rows, :].astype(bf16)


def gather_tile(refs, table_ref, target, at, tile, count, slots_per, rows):
    tiles = count // 8
    for row in rows:
        a, slot = divmod(row, slots_per)
        index = refs.index[slot * count + a * tiles + tile]
        target[pl.ds(at + row, 1), :] = table_ref[pl.ds(index, 1), :]


def sub_block(refs, source_ref, gathered, tile, width, mask, slots_per):
    lanes = gathered.shape[1]
    tiles = source_ref.shape[0] // 8
    size = width * lanes
    upright = [refs.upright[tile + u] for u in range(width)]
    pairs = [refs.pair[tile + u] for u in range(width)]
    stacked = jnp.concatenate(upright, axis=0)
    first = product(stacked, refs.first[...])
    grams = [product(upright[u][:, :16], pairs[u]) for u in range(width)]
    yield
    grams = [(x.astype(bf16) * mask) for x in grams]
    backs = [x.T for x in grams]
    source = jnp.concatenate(
        [
            jnp.broadcast_to(source_ref[pl.ds(a * tiles + tile + u, 1), :], (slots_per, lanes))
            for u in range(width)
            for a in range(8)
        ],
        axis=0,
    )
    half = first[:, :lanes] + source + gathered[...]
    flow = first[:, lanes:]
    value, slope = gate_of(half)
    slopes = [slope]
    hidden = value.astype(bf16)
    kept = [hidden]
    yield
    for layer in range(2):
        around = jnp.concatenate(
            [
                product(grams[u], hidden[u * lanes : (u + 1) * lanes]).astype(bf16)
                for u in range(width)
            ],
            axis=0,
        )
        yield
        half = product(jnp.concatenate([hidden, around], axis=1), refs.forward[layer])
        yield
        value, slope = gate_of(half)
        hidden = value.astype(bf16)
        slopes.append(slope)
        kept.append(hidden)
        yield
    turns = []
    for layer in (1, 0):
        mixed_grad = (flow * slopes[layer + 1]).astype(bf16)
        back = product(mixed_grad, refs.backward[layer])
        yield
        turn = back[:, lanes:].astype(bf16)
        turns.append(turn)
        flow = back[:, :lanes] + jnp.concatenate(
            [
                product(backs[u], turn[u * lanes : (u + 1) * lanes])
                for u in range(width)
            ],
            axis=0,
        )
        yield
    paired_grad = (flow * slopes[0]).astype(bf16)
    turns = jnp.concatenate(turns, axis=1)
    inputs = jnp.concatenate([kept[1], kept[0]], axis=1)
    cross = []
    for u in range(width):
        rows = slice(u * lanes, (u + 1) * lanes)
        cross.append(product_nt(turns[rows], inputs[rows]))
    ends = product_nt(refs.last[...], jnp.concatenate([paired_grad, kept[2]], axis=1))
    yield
    cross = [x.astype(bf16) * mask for x in cross]
    for u in range(width):
        first_row = pl.multiple_of((tile + u) * 96, 96)
        refs.results[pl.ds(first_row, 32), :] = ends[:, u * lanes : (u + 1) * lanes]
        lead = refs.lead[tile + u]
        refs.results[pl.ds(first_row + 32, 32), :] = product(lead, cross[u])
        refs.results[pl.ds(first_row + 64, 32), :] = product_nt(lead, cross[u])


def main_loop(refs, table_ref, source_ref, slots_per, width, blocks):
    count, lanes = source_ref.shape
    tiles = count // 8
    step = width * blocks
    rows = lax.broadcasted_iota(jnp.int32, (lanes, lanes), 0) // slots_per
    cols = lax.broadcasted_iota(jnp.int32, (lanes, lanes), 1) // slots_per
    refs.mask[...] = jnp.where(rows == cols, 1.0, 0.0).astype(bf16)

    for tile in range(step):
        gather_tile(
            refs, table_ref, refs.gathered, tile * lanes, tile, count, slots_per, range(lanes)
        )

    @pl.loop(0, tiles // step)
    def _(turn):
        tile = turn * step
        after = jnp.minimum(tile + step, tiles - step)
        mask = refs.mask[...]
        lanes_of = [
            sub_block(
                refs,
                source_ref,
                refs.gathered.at[b * width * lanes : (b + 1) * width * lanes],
                tile + b * width,
                width,
                mask,
                slots_per,
            )
            for b in range(blocks)
        ]
        jobs = []
        for t in range(step):
            for part in range(0, lanes, 32):
                jobs.append((t, range(part, part + 32)))
        live = True
        stage = 0
        while live:
            live = False
            for lane in lanes_of:
                for _ in lane:
                    live = True
                    break
            stage += 1
            if stage >= 2:
                for t, part in jobs[:6]:
                    gather_tile(
                        refs, table_ref, refs.gathered, t * lanes, after + t, count,
                        slots_per, part,
                    )
                jobs = jobs[6:]
        for t, part in jobs:
            gather_tile(
                refs, table_ref, refs.gathered, t * lanes, after + t, count, slots_per, part
            )


def finish(refs, scatter_ref, basis):
    tiles, lanes = refs.listed.shape
    groups = scatter_ref.shape[0] // 3
    scatter_ref[...] = jnp.zeros(scatter_ref.shape, f32)

    @pl.loop(0, tiles // 8, unroll=2)
    def _(group):
        rows = pl.ds(pl.multiple_of(8 * group, 8), 8)
        offsets = [refs.dense[k, rows, :] for k in range(3)]
        length, sine, cosine = [refs.dense[3 + k, rows, :] for k in range(3)]
        first = group * (8 * 96)

        def taken(row):
            return refs.results[pl.ds(first + row, 8, stride=96), :]

        inverse = 1.0 / length
        scaled = length / cutoff
        under = 1.0 - scaled * scaled
        smooth = under * under
        direction = [offsets[k] * inverse for k in range(3)]
        sin_before, sin_now = (jnp.zeros_like(sine), sine)
        cos_before, cos_now = (jnp.ones_like(sine), cosine)
        first_sum = jnp.zeros_like(sine)
        second_sum = jnp.zeros_like(sine)
        for b in range(basis):
            grad = taken(b) + taken(basis + b)
            first_sum = first_sum + grad * sin_now
            second_sum = second_sum + grad * (cos_now * ((b + 1) * math.pi / cutoff))
            sin_before, sin_now = (sin_now, 2.0 * cosine * sin_now - sin_before)
            cos_before, cos_now = (cos_now, 2.0 * cosine * cos_now - cos_before)
        edge_energy = taken(16)
        left = [2.0 * (taken(32 + k) + taken(38 + k)) for k in range(3)]
        right = [2.0 * (taken(64 + 9 + k) + taken(64 + 15 + k)) for k in range(3)]
        inner = left[0] * direction[0] + left[1] * direction[1] + left[2] * direction[2]
        turn = [right[k] + smooth * left[k] for k in range(3)]
        smooth_grad = inner + edge_energy + first_sum * inverse
        along = turn[0] * direction[0] + turn[1] * direction[1] + turn[2] * direction[2]
        length_grad = smooth * inverse * (second_sum - first_sum * inverse)
        length_grad = length_grad - smooth_grad * under * (2.0 * scaled / cutoff) * 2.0
        length_grad = length_grad - along * inverse
        for k in range(3):
            refs.dense[k, rows, :] = turn[k] * inverse + length_grad * direction[k]
        refs.dense[3, rows, :] = edge_energy * smooth

    @pl.loop(0, tiles // 2, unroll=4)
    def _(pair):
        tile = 2 * pair
        in_group = group_of(refs, tile, groups, 2)
        pieces = []
        for k in range(3):
            grad = jnp.concatenate(
                [refs.dense[k, pl.ds(tile + u, 1), :] for u in range(2)], axis=1
            )
            pieces.append(jnp.where(in_group, jnp.broadcast_to(grad, in_group.shape), 0.0))
        spread = jnp.concatenate(pieces, axis=0)
        scatter_ref[...] += product_nt(spread.astype(bf16), refs.hot[pair])


def gather_atoms(refs, atom_ref, energy_ref, slots_per):
    tiles, lanes = refs.listed.shape
    sums = atom_rows(lanes, slots_per).astype(bf16)
    for k in range(4):
        total = jnp.zeros((16, tiles), f32)
        for piece in split_three(refs.dense[k]):
            total = total + product_nt(sums, piece.astype(bf16))
        row = jnp.concatenate([total[a : a + 1] for a in range(8)], axis=1)
        if k == 3:
            energy_ref[...] = row
        else:
            atom_ref[k : k + 1, :] = -row


def edge_scratch(count, slots_per, breadth, groups, width, blocks):
    tiles = count // 8
    return dict(
        first=pltpu.VMEM((64, 2 * breadth), bf16),
        last=pltpu.VMEM((32, 2 * breadth), bf16),
        forward=pltpu.VMEM((2, 2 * breadth, breadth), bf16),
        backward=pltpu.VMEM((2, breadth, 2 * breadth), bf16),
        split=pltpu.VMEM((6 * groups, breadth), bf16),
        listed=pltpu.VMEM((tiles, breadth), jnp.int32),
        dense=pltpu.VMEM((6, tiles, breadth), f32),
        narrow=pltpu.VMEM((tiles * 64, breadth), f32),
        pairs=pltpu.VMEM((tiles * 16, breadth), f32),
        lead=pltpu.VMEM((tiles, 32, breadth), bf16),
        upright=pltpu.VMEM((tiles, breadth, 64), bf16),
        pair=pltpu.VMEM((tiles, 16, breadth), bf16),
        gathered=pltpu.VMEM((width * blocks * breadth, breadth), f32),
        results=pltpu.VMEM((tiles * 96, breadth), f32),
        hot=pltpu.VMEM((tiles // 2, breadth, 2 * breadth), bf16),
        mask=pltpu.VMEM((breadth, breadth), bf16),
        index=pltpu.SMEM((slots_per * count,), jnp.int32),
    )


def others(shape):
    here = (lax.axis_index("gx"), lax.axis_index("gy"))
    steps = [(n // 3 - 1, n % 3 - 1) for n in range(9)]

    def at(dx, dy):
        return (
            lax.rem(here[0] + (dx + shape[0]), shape[0]),
            lax.rem(here[1] + (dy + shape[1]), shape[1]),
        )

    return (at, steps)


def greet(shape):
    at, steps = others(shape)
    barrier = pltpu.get_barrier_semaphore()
    for dx, dy in steps:
        if (dx, dy) != (0, 0):
            pl.semaphore_signal(
                barrier, inc=1, device_id=at(dx, dy), device_id_type=pl.DeviceIdType.MESH
            )
    return barrier


def send(source, landing, sems, device):
    copy = pltpu.make_async_remote_copy(
        src_ref=source,
        dst_ref=landing,
        send_sem=sems[0],
        recv_sem=sems[1],
        device_id=device,
        device_id_type=pl.DeviceIdType.MESH,
    )
    copy.start()
    return copy


def hot_columns(slots, count):
    rows = lax.broadcasted_iota(jnp.int32, (count, slots.shape[1]), 0)
    return jnp.where(rows == slots, 1.0, 0.0)


def fetch_all(pairs, sems):
    copies = [
        pltpu.make_async_copy(far, near, sems.at[n]) for n, (far, near) in enumerate(pairs)
    ]
    for copy in copies:
        copy.start()
    return copies


def whole_kernel(shape, plan, names, *operands):
    r = types.SimpleNamespace(**dict(zip(names, operands)))
    width, blocks = plan
    slots_per, count = r.neighbours.shape
    breadth = r.features.shape[1]
    sent = r.slots_x.shape[1]
    ghost_count = r.ghosts.shape[1]
    basis = r.radial.shape[0]
    own_groups = count // breadth
    ghost_groups = ghost_count // breadth
    at, steps = others(shape)
    around = [n for n, step in enumerate(steps) if step != (0, 0)]
    barrier = greet(shape)
    fetches = fetch_all(
        [
            (r.features_far, r.features),
            (r.slots_x_far, r.slots_x),
            (r.slots_y_far, r.slots_y),
            (r.ghosts_far, r.ghosts),
            (r.source_weight_far, r.source_weight),
            (r.target_weight_far, r.target_weight),
        ],
        r.fetch_sem,
    )
    lists = fetch_all(
        [
            (r.neighbours.at[slot], r.index.at[pl.ds(slot * count, count)])
            for slot in range(slots_per)
        ],
        r.index_sem,
    )
    later = fetch_all(
        [
            (r.radial_far, r.radial),
            (r.readout_far, r.readout),
            (r.environ_first_far, r.environ_first),
            (r.mixing_first_far, r.mixing_first),
            (r.coupler_first_far, r.coupler_first),
            (r.environ_second_far, r.environ_second),
            (r.mixing_second_far, r.mixing_second),
            (r.coupler_second_far, r.coupler_second),
        ],
        r.later_sem,
    )

    holding = r.holding
    blank = jnp.zeros((5, count), f32)
    pieces = []
    for piece in split_three(r.coords[...].reshape(3, count)):
        pieces += [piece, blank]
    pieces.append(jnp.zeros((breadth - 24, count), f32))
    holding[:, breadth:] = jnp.concatenate(pieces, axis=0).T.astype(bf16)
    for fetch in fetches:
        fetch.wait()
    holding[:, :breadth] = r.features[...]
    moves = [
        jnp.concatenate([n[0:1, :], n[1:2, :]], axis=1) for n in (r.slots_x, r.slots_y)
    ]
    picks = hot_columns(jnp.concatenate(moves, axis=1), count).T.astype(bf16)

    def leave(axis):
        chosen_rows = picks[2 * sent * axis : 2 * sent * (axis + 1)]
        payload = product(chosen_rows, holding[...]).astype(bf16)
        r.leaving[axis, 0] = payload[:sent]
        r.leaving[axis, 1] = payload[sent:]
        if axis == 0:
            pl.semaphore_wait(barrier, 8)
        return [
            send(
                r.leaving.at[axis, way],
                r.arriving.at[axis, way],
                (r.move_send.at[axis, way], r.move_recv.at[axis, way]),
                at(stride, 0) if axis == 0 else at(0, stride),
            )
            for way, stride in ((0, 1), (1, -1))
        ]

    def settle(axis, copies):
        put = hot_columns(moves[axis], count)
        hit = jnp.max(put, axis=1, keepdims=True) > 0.5
        for copy in copies:
            copy.wait()
        came = r.arriving[axis].reshape(2 * sent, 2 * breadth)
        moved = product(put.astype(bf16), came)
        holding[...] = jnp.where(hit, moved, holding[...].astype(f32)).astype(bf16)

    copies = leave(0)
    for fetch in later:
        fetch.wait()
    prepare_weights(
        r,
        (
            r.radial,
            (r.environ_first, r.environ_second),
            (r.mixing_first, r.mixing_second),
            (r.coupler_first, r.coupler_second),
            r.readout,
        ),
        1.0 / math.sqrt(slots_per),
    )
    settle(0, copies)
    copies = leave(1)
    prepare_lists(r, r.neighbours)
    ghost_hot = hot_columns(r.ghosts[...], count)
    ghost_picks = ghost_hot.T.astype(bf16)
    ghost_hot = ghost_hot.astype(bf16)
    settle(1, copies)

    flat = holding[:, breadth:].astype(f32).T[:24]
    ghost_flat = product(flat.astype(bf16), ghost_hot)
    ghost_places = ghost_flat[:8] + ghost_flat[8:16] + ghost_flat[16:24]
    r.ghost_places[...] = ghost_places[:4]
    waits = {}
    for n in around:
        dx, dy = steps[n]
        waits[n] = [
            send(
                r.ghost_places,
                r.halo_places.at[n],
                (r.places_send.at[n], r.places_recv.at[n]),
                at(-dx, -dy),
            )
        ]
    rows = holding[:, :breadth]
    half_target = (0.5 * r.target_weight[...].astype(f32)).astype(bf16)
    half_source = (0.5 * r.source_weight[...].astype(f32)).astype(bf16)
    target = product(rows, half_target).astype(bf16)
    chunks = [pl.ds(c * (ghost_count // 2), ghost_count // 2) for c in range(2)]

    def send_rows(source, n, c, device):
        return send(
            source.at[chunks[c]],
            r.halo_rows.at[n, chunks[c]],
            (r.rows_send.at[n, c], r.rows_recv.at[n, c]),
            device,
        )

    cross = {}
    for c in range(2):
        part = slice(c * (ghost_count // 2), (c + 1) * (ghost_count // 2))
        r.ghost_rows[part] = product(ghost_picks[part], target).astype(bf16)
        for n in (1, 7):
            cross[n, c] = send_rows(r.ghost_rows, n, c, at(-steps[n][0], 0))
    for c in range(2):
        for n in (3, 5):
            waits[n].append(send_rows(r.ghost_rows, n, c, at(0, -steps[n][1])))

    r.table[:count, :] = target.astype(f32)
    r.source[...] = product(rows, half_source).astype(bf16).astype(f32)
    mine = flat[:8] + flat[8:16] + flat[16:24]
    r.own[...] = mine
    place = r.place
    place[...] = jnp.zeros(place.shape, f32)
    for k in range(3):
        for g in range(own_groups):
            place[k, g : g + 1, :] = mine[k : k + 1, g * breadth : (g + 1) * breadth]
    rows_at = pl.ds(count + 4 * ghost_count, ghost_count)
    r.table[rows_at, :] = jnp.zeros((ghost_count, breadth), f32)

    r.give[...] = jnp.zeros(r.give.shape, f32)
    for c in range(2):
        for n in (1, 7):
            cross[n, c].wait()
            for dy in (-1, 1):
                waits[n + dy].append(send_rows(r.halo_rows.at[n], n + dy, c, at(0, -dy)))
    for n in around:
        waits[n][0].wait()
        places = r.halo_places[n]
        for k in range(3):
            for g in range(ghost_groups):
                group = own_groups + n * ghost_groups + g
                place[k, group : group + 1, :] = places[
                    k : k + 1, g * breadth : (g + 1) * breadth
                ]
    prepare_places(r, place)
    geometry(r, r.own, basis, slots_per)
    spread_tiles(r)
    for copy in lists:
        copy.wait()
    for n in around:
        for copy in waits[n][1:]:
            copy.wait()
        rows_at = pl.ds(count + n * ghost_count, ghost_count)
        r.table[rows_at, :] = r.halo_rows[n].astype(f32)

    main_loop(r, r.table, r.source, slots_per, width, blocks)
    finish(r, r.scatter, basis)

    scatter = r.scatter
    groups = scatter.shape[0] // 3
    for n in range(9):
        for g in range(ghost_groups):
            group = own_groups + n * ghost_groups + g
            for k in range(3):
                r.give[n, k : k + 1, g * breadth : (g + 1) * breadth] = scatter[
                    pl.ds(k * groups + group, 1), :
                ]
    copies = {}
    for n in around:
        copies[n] = send(
            r.give.at[n], r.got.at[n], (r.give_send.at[n], r.give_recv.at[n]),
            at(*steps[n]),
        )
    gather_atoms(r, r.by_atom, r.energy, slots_per)
    spots = hot_columns(r.ghosts[...], count).T.astype(bf16)
    owns = []
    for k in range(3):
        own = jnp.concatenate(
            [scatter[pl.ds(k * groups + g, 1), :] for g in range(own_groups)], axis=1
        )
        owns.append(own + r.by_atom[k : k + 1, :])
    total = r.give[4][:3]
    for n in around:
        copies[n].wait()
        total = total + r.got[n][:3]
    stack = jnp.concatenate(
        [jnp.concatenate([x, jnp.zeros((5, ghost_count), f32)], axis=0) for x in split_three(total)],
        axis=0,
    ).astype(bf16)
    back = product(stack, spots)
    back = back[:8] + back[8:16] + back[16:24]
    for k in range(3):
        r.force[k] = -(owns[k] + back[k : k + 1, :])


def per_device(
    shape,
    features,
    coords,
    migrate_x_slots,
    migrate_y_slots,
    ghost_slots,
    neighbours,
    source_weight,
    target_weight,
    radial_weight,
    environ_first,
    mixing_first,
    coupler_first,
    environ_second,
    mixing_second,
    coupler_second,
    readout,
):
    features = features[0, 0]
    count, breadth = features.shape
    coords = coords.transpose(0, 2, 1, 3).reshape(3, 1, count)
    neighbours = neighbours[0, 0].T
    ghosts = ghost_slots.reshape(1, -1)
    slots_per = neighbours.shape[0]
    ghost_count = ghosts.shape[1]
    sent = migrate_x_slots.shape[3]
    total_rows = count + 9 * ghost_count
    groups = -(-(total_rows // breadth) // 8) * 8
    width, blocks = 4, 4
    vmem = pl.BlockSpec(memory_space=pltpu.VMEM)
    hbm = pl.BlockSpec(memory_space=pltpu.HBM)
    dma = pltpu.SemaphoreType.DMA
    square = pltpu.VMEM((breadth, breadth), bf16)
    inputs = dict(
        features_far=features,
        coords=coords,
        slots_x_far=migrate_x_slots[0, 0],
        slots_y_far=migrate_y_slots[0, 0],
        ghosts_far=ghosts,
        neighbours=neighbours,
        source_weight_far=source_weight,
        target_weight_far=target_weight,
        radial_far=radial_weight,
        environ_first_far=environ_first,
        mixing_first_far=mixing_first,
        coupler_first_far=coupler_first,
        environ_second_far=environ_second,
        mixing_second_far=mixing_second,
        coupler_second_far=coupler_second,
        readout_far=readout[None],
    )
    scratch = dict(
        features=pltpu.VMEM((count, breadth), bf16),
        slots_x=pltpu.VMEM((2, sent), jnp.int32),
        slots_y=pltpu.VMEM((2, sent), jnp.int32),
        ghosts=pltpu.VMEM((1, ghost_count), jnp.int32),
        source_weight=square,
        target_weight=square,
        radial=pltpu.VMEM(radial_weight.shape, f32),
        readout=pltpu.VMEM((1, breadth), bf16),
        environ_first=square,
        mixing_first=square,
        coupler_first=square,
        environ_second=square,
        mixing_second=square,
        coupler_second=square,
        fetch_sem=dma((6,)),
        index_sem=dma((slots_per,)),
        later_sem=dma((8,)),
        table=pltpu.VMEM((total_rows, breadth), f32),
        source=pltpu.VMEM((count, breadth), f32),
        place=pltpu.VMEM((3, groups, breadth), f32),
        own=pltpu.VMEM((8, count), f32),
        scatter=pltpu.VMEM((3 * groups, breadth), f32),
        by_atom=pltpu.VMEM((8, count), f32),
        holding=pltpu.VMEM((count, 2 * breadth), bf16),
        leaving=pltpu.VMEM((2, 2, sent, 2 * breadth), bf16),
        arriving=pltpu.VMEM((2, 2, sent, 2 * breadth), bf16),
        ghost_rows=pltpu.VMEM((ghost_count, breadth), bf16),
        ghost_places=pltpu.VMEM((4, ghost_count), f32),
        halo_rows=pltpu.VMEM((9, ghost_count, breadth), bf16),
        halo_places=pltpu.VMEM((9, 4, ghost_count), f32),
        give=pltpu.VMEM((9, 4, ghost_count), f32),
        got=pltpu.VMEM((9, 4, ghost_count), f32),
        move_send=dma((2, 2)),
        move_recv=dma((2, 2)),
        rows_send=dma((9, 2)),
        rows_recv=dma((9, 2)),
        places_send=dma((9,)),
        places_recv=dma((9,)),
        give_send=dma((9,)),
        give_recv=dma((9,)),
        **edge_scratch(count, slots_per, breadth, groups, width, blocks),
    )
    names = tuple(inputs) + ("force", "energy") + tuple(scratch)
    forces, energies = pl.pallas_call(
        functools.partial(whole_kernel, shape, (width, blocks), names),
        out_shape=(
            jax.ShapeDtypeStruct((3, 1, count), f32),
            jax.ShapeDtypeStruct((1, count), f32),
        ),
        in_specs=[vmem if n in ("coords", "neighbours") else hbm for n in inputs],
        out_specs=(vmem,) * 2,
        scratch_shapes=list(scratch.values()),
        compiler_params=pltpu.CompilerParams(
            collective_id=0, has_side_effects=True, vmem_limit_bytes=67043328
        ),
        name="allegro",
    )(*inputs.values())
    return (forces.reshape(1, 3, 1, count).transpose(0, 2, 1, 3), energies[None])


def solution(mesh):
    in_specs = (
        P("gx", "gy", None, None),
        P("gx", "gy", None, None),
        P("gx", "gy", None, None),
        P("gx", "gy", None, None),
        P("gx", "gy", None),
        P("gx", "gy", None, None),
        P(),
        P(),
        P(),
        P(),
        P(),
        P(),
        P(),
        P(),
        P(),
        P(),
    )
    out_specs = (P("gx", "gy", None, None), P("gx", "gy", None))
    return jax.shard_map(
        functools.partial(per_device, (mesh.shape["gx"], mesh.shape["gy"])),
        mesh=mesh, in_specs=in_specs, out_specs=out_specs, check_vma=False
    )
```

```python
import functools
import math
import types

import jax
import jax.numpy as jnp
from jax import lax
from jax.experimental import pallas as pl
from jax.experimental.pallas import tpu as pltpu
from jax.sharding import PartitionSpec as P

soften = 0.25
cutoff = 2.0
f32 = jnp.float32
bf16 = jnp.bfloat16


def split_two(value):
    top = value.astype(bf16).astype(f32)
    return (top, value - top)


def split_three(value):
    top = value.astype(bf16).astype(f32)
    rest = value - top
    middle = rest.astype(bf16).astype(f32)
    return (top, middle, rest - middle)


def turned(weight):
    return weight.astype(f32).T.astype(bf16)


def product(left, right):
    return jnp.dot(left, right, preferred_element_type=f32)


def product_nt(left, right):
    return lax.dot_general(left, right, (((1,), (1,)), ((), ())), preferred_element_type=f32)


def product_tn(left, right):
    return lax.dot_general(left, right, (((0,), (0,)), ((), ())), preferred_element_type=f32)


def gate_of(half):
    lift = 1.0 + jnp.tanh(half)
    value = half * lift
    return value, lift + value * (2.0 - lift)


def prepare_weights(refs, weights, norm_scale):
    (radial_ref, environ, mixing, coupler, readout_ref) = weights
    breadth = radial_ref.shape[1]
    basis = radial_ref.shape[0]
    w_top, w_low = split_two(radial_ref[...])
    row = readout_ref[...].astype(f32)
    blank = functools.partial(jnp.zeros, dtype=f32)
    left = jnp.concatenate([blank((32, breadth)), w_top, w_low, w_top, blank((8, breadth))], axis=0)
    right = jnp.concatenate(
        [blank((32 + 3 * basis, breadth)), row, row, blank((6, breadth))], axis=0
    )
    refs.first[:, :breadth] = (0.5 * left).astype(bf16)
    refs.first[:, breadth:] = (0.5 * right).astype(bf16)
    last = jnp.concatenate(
        [
            jnp.concatenate([w_top, w_low, blank((16, breadth))], axis=0),
            jnp.concatenate([blank((16, breadth)), row, blank((15, breadth))], axis=0),
        ],
        axis=1,
    )
    refs.last[...] = last.astype(bf16)
    for layer in range(2):
        joined = product(environ[layer][...], coupler[layer][...]) * (0.5 * norm_scale)
        mixed = 0.5 * mixing[layer][...].astype(f32)
        refs.forward[layer, :breadth, :] = mixed.astype(bf16)
        refs.forward[layer, breadth:, :] = joined.astype(bf16)
        refs.backward[layer, :, :breadth] = mixed.T.astype(bf16)
        refs.backward[layer, :, breadth:] = joined.T.astype(bf16)


def prepare_places(refs, place_ref):
    breadth = place_ref.shape[2]
    places = place_ref[...].reshape(-1, breadth)
    refs.split[...] = jnp.concatenate(split_two(places), axis=0).astype(bf16)


def prepare_lists(refs, neighbours):
    slots_per, count = neighbours.shape
    tiles = count // 8
    listed = neighbours[...].astype(f32)
    rows = jnp.concatenate([listed[:, a * tiles : (a + 1) * tiles] for a in range(8)], axis=0)
    refs.listed[...] = rows.T.astype(jnp.int32)


def atom_rows(lanes, slots_per):
    rows = lax.broadcasted_iota(jnp.int32, (16, lanes), 0)
    cols = lax.broadcasted_iota(jnp.int32, (16, lanes), 1)
    return jnp.where(rows == cols // slots_per, 1.0, 0.0)


def index_of(refs, tile, width):
    return jnp.concatenate([refs.listed[pl.ds(tile + u, 1), :] for u in range(width)], axis=1)


def group_of(refs, tile, groups, width):
    breadth = refs.listed.shape[1]
    high = index_of(refs, tile, width) >> (breadth.bit_length() - 1)
    return lax.broadcasted_iota(jnp.int32, (groups, width * breadth), 0) == high


def hot_of(refs, tile, width):
    breadth = refs.listed.shape[1]
    low = index_of(refs, tile, width) & (breadth - 1)
    rows = lax.broadcasted_iota(jnp.int32, (breadth, width * breadth), 0)
    return jnp.where(rows == low, 1.0, 0.0).astype(bf16)


def geometry(refs, own_ref, basis, slots_per):
    tiles, lanes = refs.listed.shape
    groups = refs.split.shape[0] // 6
    size = 3 * groups
    spread = atom_rows(lanes, slots_per)[:8]
    spread = jnp.concatenate([spread] * 3, axis=0).astype(bf16)
    for k in range(3):
        own = jnp.concatenate(
            [own_ref[k : k + 1, a * tiles : (a + 1) * tiles] for a in range(8)], axis=0
        )
        own = jnp.concatenate(split_three(own), axis=0).astype(bf16)
        refs.dense[3 + k] = product_tn(own, spread)

    @pl.loop(0, tiles // 2, unroll=4)
    def _(pair):
        tile = 2 * pair
        one_hot = hot_of(refs, tile, 2)
        in_group = group_of(refs, tile, groups, 2)
        refs.hot[pair] = one_hot
        found = product(refs.split[...], one_hot)
        found = found[:size] + found[size:]
        for k in range(3):
            far = jnp.sum(
                jnp.where(in_group, found[k * groups : (k + 1) * groups], 0.0),
                axis=0,
                keepdims=True,
            )
            for u in range(2):
                refs.dense[k, pl.ds(tile + u, 1), :] = far[:, u * lanes : (u + 1) * lanes]

    @pl.loop(0, tiles // 8, unroll=2)
    def _(group):
        rows = pl.ds(pl.multiple_of(8 * group, 8), 8)
        offsets = [refs.dense[k, rows, :] - refs.dense[3 + k, rows, :] for k in range(3)]
        square = offsets[0] * offsets[0] + offsets[1] * offsets[1] + offsets[2] * offsets[2]
        length = jnp.sqrt(square + soften)
        inverse = 1.0 / length
        scaled = length / cutoff
        smooth = (1.0 - scaled * scaled) ** 2
        angle = scaled * math.pi
        sine = jnp.sin(angle)
        cosine = jnp.cos(angle)
        factor = inverse * smooth
        for n, value in enumerate(offsets + [length, sine, cosine]):
            refs.dense[n, rows, :] = value
        direction = [offsets[k] * inverse for k in range(3)]
        weighted = [direction[k] * smooth for k in range(3)]
        d_top, d_low = zip(*[split_two(x) for x in direction])
        w_top, w_low = zip(*[split_two(x) for x in weighted])
        before, now = (jnp.zeros_like(sine), sine)
        b_top, b_low = [], []
        for _ in range(basis):
            top, low = split_two(now * factor)
            b_top.append(top)
            b_low.append(low)
            before, now = (now, 2.0 * cosine * now - before)
        s_top, s_low = split_two(smooth)
        blank = jnp.zeros_like(sine)
        left = list(d_top) * 2 + list(d_low) + list(w_top) * 2 + list(w_low) + [blank] * 14
        right = list(w_top) + list(w_low) + list(w_top)
        values = left + b_top + b_top + b_low + [s_top, s_low] + [blank] * 6
        for n, value in enumerate(values):
            start = pl.multiple_of(group * 512 + n * 8, 8)
            refs.narrow[pl.ds(start, 8), :] = value
        for n in range(16):
            start = pl.multiple_of(group * 128 + n * 8, 8)
            refs.pairs[pl.ds(start, 8), :] = right[n] if n < 9 else blank


def spread_tiles(refs):
    tiles = refs.listed.shape[0]

    @pl.loop(0, tiles // 8, unroll=2)
    def _(group):
        for member in range(8):
            tile = group * 8 + member
            whole = refs.narrow[pl.ds(group * 512 + member, 64, stride=8), :].astype(bf16)
            rows = pl.ds(group * 128 + member, 16, stride=8)
            refs.lead[tile] = whole[:32]
            refs.upright[tile] = whole.T
            refs.pair[tile] = refs.pairs[rows, :].astype(bf16)


def gather_tile(refs, table_ref, target, at, tile, count, slots_per, rows):
    tiles = count // 8
    for row in rows:
        a, slot = divmod(row, slots_per)
        index = refs.index[slot * count + a * tiles + tile]
        target[pl.ds(at + row, 1), :] = table_ref[pl.ds(index, 1), :]


def sub_block(refs, source_ref, gathered, tile, width, mask, slots_per):
    lanes = gathered.shape[1]
    tiles = source_ref.shape[0] // 8
    size = width * lanes
    upright = [refs.upright[tile + u] for u in range(width)]
    pairs = [refs.pair[tile + u] for u in range(width)]
    stacked = jnp.concatenate(upright, axis=0)
    first = product(stacked, refs.first[...])
    grams = [product(upright[u][:, :16], pairs[u]) for u in range(width)]
    yield
    grams = [(x.astype(bf16) * mask) for x in grams]
    backs = [x.T for x in grams]
    source = jnp.concatenate(
        [
            jnp.broadcast_to(source_ref[pl.ds(a * tiles + tile + u, 1), :], (slots_per, lanes))
            for u in range(width)
            for a in range(8)
        ],
        axis=0,
    )
    half = first[:, :lanes] + source + gathered[...]
    flow = first[:, lanes:]
    value, slope = gate_of(half)
    slopes = [slope]
    hidden = value.astype(bf16)
    kept = [hidden]
    yield
    for layer in range(2):
        around = jnp.concatenate(
            [
                product(grams[u], hidden[u * lanes : (u + 1) * lanes]).astype(bf16)
                for u in range(width)
            ],
            axis=0,
        )
        yield
        half = product(jnp.concatenate([hidden, around], axis=1), refs.forward[layer])
        yield
        value, slope = gate_of(half)
        hidden = value.astype(bf16)
        slopes.append(slope)
        kept.append(hidden)
        yield
    turns = []
    for layer in (1, 0):
        mixed_grad = (flow * slopes[layer + 1]).astype(bf16)
        back = product(mixed_grad, refs.backward[layer])
        yield
        turn = back[:, lanes:].astype(bf16)
        turns.append(turn)
        flow = back[:, :lanes] + jnp.concatenate(
            [
                product(backs[u], turn[u * lanes : (u + 1) * lanes])
                for u in range(width)
            ],
            axis=0,
        )
        yield
    paired_grad = (flow * slopes[0]).astype(bf16)
    turns = jnp.concatenate(turns, axis=1)
    inputs = jnp.concatenate([kept[1], kept[0]], axis=1)
    cross = []
    for u in range(width):
        rows = slice(u * lanes, (u + 1) * lanes)
        cross.append(product_nt(turns[rows], inputs[rows]))
    ends = product_nt(refs.last[...], jnp.concatenate([paired_grad, kept[2]], axis=1))
    yield
    cross = [x.astype(bf16) * mask for x in cross]
    for u in range(width):
        first_row = pl.multiple_of((tile + u) * 96, 96)
        refs.results[pl.ds(first_row, 32), :] = ends[:, u * lanes : (u + 1) * lanes]
        lead = refs.lead[tile + u]
        refs.results[pl.ds(first_row + 32, 32), :] = product(lead, cross[u])
        refs.results[pl.ds(first_row + 64, 32), :] = product_nt(lead, cross[u])


def main_loop(refs, table_ref, source_ref, slots_per, width, blocks):
    count, lanes = source_ref.shape
    tiles = count // 8
    step = width * blocks
    rows = lax.broadcasted_iota(jnp.int32, (lanes, lanes), 0) // slots_per
    cols = lax.broadcasted_iota(jnp.int32, (lanes, lanes), 1) // slots_per
    refs.mask[...] = jnp.where(rows == cols, 1.0, 0.0).astype(bf16)

    for tile in range(step):
        gather_tile(
            refs, table_ref, refs.gathered, tile * lanes, tile, count, slots_per, range(lanes)
        )

    @pl.loop(0, tiles // step)
    def _(turn):
        tile = turn * step
        after = jnp.minimum(tile + step, tiles - step)
        mask = refs.mask[...]
        lanes_of = [
            sub_block(
                refs,
                source_ref,
                refs.gathered.at[b * width * lanes : (b + 1) * width * lanes],
                tile + b * width,
                width,
                mask,
                slots_per,
            )
            for b in range(blocks)
        ]
        jobs = []
        for t in range(step):
            for part in range(0, lanes, 32):
                jobs.append((t, range(part, part + 32)))
        live = True
        stage = 0
        while live:
            live = False
            for lane in lanes_of:
                for _ in lane:
                    live = True
                    break
            stage += 1
            if stage >= 2:
                for t, part in jobs[:6]:
                    gather_tile(
                        refs, table_ref, refs.gathered, t * lanes, after + t, count,
                        slots_per, part,
                    )
                jobs = jobs[6:]
        for t, part in jobs:
            gather_tile(
                refs, table_ref, refs.gathered, t * lanes, after + t, count, slots_per, part
            )


def finish(refs, scatter_ref, basis):
    tiles, lanes = refs.listed.shape
    groups = scatter_ref.shape[0] // 3
    scatter_ref[...] = jnp.zeros(scatter_ref.shape, f32)

    @pl.loop(0, tiles // 8, unroll=2)
    def _(group):
        rows = pl.ds(pl.multiple_of(8 * group, 8), 8)
        offsets = [refs.dense[k, rows, :] for k in range(3)]
        length, sine, cosine = [refs.dense[3 + k, rows, :] for k in range(3)]
        first = group * (8 * 96)

        def taken(row):
            return refs.results[pl.ds(first + row, 8, stride=96), :]

        inverse = 1.0 / length
        scaled = length / cutoff
        under = 1.0 - scaled * scaled
        smooth = under * under
        direction = [offsets[k] * inverse for k in range(3)]
        sin_before, sin_now = (jnp.zeros_like(sine), sine)
        cos_before, cos_now = (jnp.ones_like(sine), cosine)
        first_sum = jnp.zeros_like(sine)
        second_sum = jnp.zeros_like(sine)
        for b in range(basis):
            grad = taken(b) + taken(basis + b)
            first_sum = first_sum + grad * sin_now
            second_sum = second_sum + grad * (cos_now * ((b + 1) * math.pi / cutoff))
            sin_before, sin_now = (sin_now, 2.0 * cosine * sin_now - sin_before)
            cos_before, cos_now = (cos_now, 2.0 * cosine * cos_now - cos_before)
        edge_energy = taken(16)
        left = [2.0 * (taken(32 + k) + taken(38 + k)) for k in range(3)]
        right = [2.0 * (taken(64 + 9 + k) + taken(64 + 15 + k)) for k in range(3)]
        inner = left[0] * direction[0] + left[1] * direction[1] + left[2] * direction[2]
        turn = [right[k] + smooth * left[k] for k in range(3)]
        smooth_grad = inner + edge_energy + first_sum * inverse
        along = turn[0] * direction[0] + turn[1] * direction[1] + turn[2] * direction[2]
        length_grad = smooth * inverse * (second_sum - first_sum * inverse)
        length_grad = length_grad - smooth_grad * under * (2.0 * scaled / cutoff) * 2.0
        length_grad = length_grad - along * inverse
        for k in range(3):
            refs.dense[k, rows, :] = turn[k] * inverse + length_grad * direction[k]
        refs.dense[3, rows, :] = edge_energy * smooth

    @pl.loop(0, tiles // 2, unroll=4)
    def _(pair):
        tile = 2 * pair
        in_group = group_of(refs, tile, groups, 2)
        pieces = []
        for k in range(3):
            grad = jnp.concatenate(
                [refs.dense[k, pl.ds(tile + u, 1), :] for u in range(2)], axis=1
            )
            pieces.append(jnp.where(in_group, jnp.broadcast_to(grad, in_group.shape), 0.0))
        spread = jnp.concatenate(pieces, axis=0)
        scatter_ref[...] += product_nt(spread.astype(bf16), refs.hot[pair])


def gather_atoms(refs, atom_ref, energy_ref, slots_per):
    tiles, lanes = refs.listed.shape
    sums = atom_rows(lanes, slots_per).astype(bf16)
    for k in range(4):
        total = jnp.zeros((16, tiles), f32)
        for piece in split_three(refs.dense[k]):
            total = total + product_nt(sums, piece.astype(bf16))
        row = jnp.concatenate([total[a : a + 1] for a in range(8)], axis=1)
        if k == 3:
            energy_ref[...] = row
        else:
            atom_ref[k : k + 1, :] = -row


def edge_scratch(count, slots_per, breadth, groups, width, blocks):
    tiles = count // 8
    return dict(
        first=pltpu.VMEM((64, 2 * breadth), bf16),
        last=pltpu.VMEM((32, 2 * breadth), bf16),
        forward=pltpu.VMEM((2, 2 * breadth, breadth), bf16),
        backward=pltpu.VMEM((2, breadth, 2 * breadth), bf16),
        split=pltpu.VMEM((6 * groups, breadth), bf16),
        listed=pltpu.VMEM((tiles, breadth), jnp.int32),
        dense=pltpu.VMEM((6, tiles, breadth), f32),
        narrow=pltpu.VMEM((tiles * 64, breadth), f32),
        pairs=pltpu.VMEM((tiles * 16, breadth), f32),
        lead=pltpu.VMEM((tiles, 32, breadth), bf16),
        upright=pltpu.VMEM((tiles, breadth, 64), bf16),
        pair=pltpu.VMEM((tiles, 16, breadth), bf16),
        gathered=pltpu.VMEM((width * blocks * breadth, breadth), f32),
        results=pltpu.VMEM((tiles * 96, breadth), f32),
        hot=pltpu.VMEM((tiles // 2, breadth, 2 * breadth), bf16),
        mask=pltpu.VMEM((breadth, breadth), bf16),
        index=pltpu.SMEM((slots_per * count,), jnp.int32),
    )


def others(shape):
    here = (lax.axis_index("gx"), lax.axis_index("gy"))
    steps = [(n // 3 - 1, n % 3 - 1) for n in range(9)]

    def at(dx, dy):
        return (
            lax.rem(here[0] + (dx + shape[0]), shape[0]),
            lax.rem(here[1] + (dy + shape[1]), shape[1]),
        )

    return (at, steps)


def greet(shape):
    at, steps = others(shape)
    barrier = pltpu.get_barrier_semaphore()
    for dx, dy in steps:
        if (dx, dy) != (0, 0):
            pl.semaphore_signal(
                barrier, inc=1, device_id=at(dx, dy), device_id_type=pl.DeviceIdType.MESH
            )
    return barrier


def send(source, landing, sems, device):
    copy = pltpu.make_async_remote_copy(
        src_ref=source,
        dst_ref=landing,
        send_sem=sems[0],
        recv_sem=sems[1],
        device_id=device,
        device_id_type=pl.DeviceIdType.MESH,
    )
    copy.start()
    return copy


def hot_columns(slots, count):
    rows = lax.broadcasted_iota(jnp.int32, (count, slots.shape[1]), 0)
    return jnp.where(rows == slots, 1.0, 0.0)


def fetch_all(pairs, sems):
    copies = [
        pltpu.make_async_copy(far, near, sems.at[n]) for n, (far, near) in enumerate(pairs)
    ]
    for copy in copies:
        copy.start()
    return copies


def whole_kernel(shape, plan, names, *operands):
    r = types.SimpleNamespace(**dict(zip(names, operands)))
    width, blocks = plan
    slots_per, count = r.neighbours.shape
    breadth = r.features.shape[1]
    sent = r.slots_x.shape[1]
    ghost_count = r.ghosts.shape[1]
    basis = r.radial.shape[0]
    own_groups = count // breadth
    ghost_groups = ghost_count // breadth
    at, steps = others(shape)
    around = [n for n, step in enumerate(steps) if step != (0, 0)]
    barrier = greet(shape)
    fetches = fetch_all(
        [
            (r.features_far, r.features),
            (r.slots_x_far, r.slots_x),
            (r.slots_y_far, r.slots_y),
            (r.ghosts_far, r.ghosts),
            (r.source_weight_far, r.source_weight),
            (r.target_weight_far, r.target_weight),
            (r.coords_far, r.coords),
            (r.neighbours_far, r.neighbours),
        ],
        r.fetch_sem,
    )
    later = fetch_all(
        [
            (r.radial_far, r.radial),
            (r.readout_far, r.readout),
            (r.environ_first_far, r.environ_first),
            (r.mixing_first_far, r.mixing_first),
            (r.coupler_first_far, r.coupler_first),
            (r.environ_second_far, r.environ_second),
            (r.mixing_second_far, r.mixing_second),
            (r.coupler_second_far, r.coupler_second),
        ],
        r.later_sem,
    )

    for fetch in fetches:
        fetch.wait()
    lists = fetch_all(
        [
            (r.neighbours.at[slot], r.index.at[pl.ds(slot * count, count)])
            for slot in range(slots_per)
        ],
        r.index_sem,
    )
    holding = r.holding
    blank = jnp.zeros((5, count), f32)
    pieces = []
    for piece in split_three(r.coords[...].reshape(3, count)):
        pieces += [piece, blank]
    pieces.append(jnp.zeros((breadth - 24, count), f32))
    holding[:, breadth:] = jnp.concatenate(pieces, axis=0).T.astype(bf16)
    holding[:, :breadth] = r.features[...]
    moves = [
        jnp.concatenate([n[0:1, :], n[1:2, :]], axis=1) for n in (r.slots_x, r.slots_y)
    ]
    picks = hot_columns(jnp.concatenate(moves, axis=1), count).T.astype(bf16)

    def leave(axis):
        chosen_rows = picks[2 * sent * axis : 2 * sent * (axis + 1)]
        payload = product(chosen_rows, holding[...]).astype(bf16)
        r.leaving[axis, 0] = payload[:sent]
        r.leaving[axis, 1] = payload[sent:]
        if axis == 0:
            pl.semaphore_wait(barrier, 8)
        return [
            send(
                r.leaving.at[axis, way],
                r.arriving.at[axis, way],
                (r.move_send.at[axis, way], r.move_recv.at[axis, way]),
                at(stride, 0) if axis == 0 else at(0, stride),
            )
            for way, stride in ((0, 1), (1, -1))
        ]

    def settle(axis, copies):
        put = hot_columns(moves[axis], count)
        hit = jnp.max(put, axis=1, keepdims=True) > 0.5
        for copy in copies:
            copy.wait()
        came = r.arriving[axis].reshape(2 * sent, 2 * breadth)
        moved = product(put.astype(bf16), came)
        holding[...] = jnp.where(hit, moved, holding[...].astype(f32)).astype(bf16)

    copies = leave(0)
    for fetch in later:
        fetch.wait()
    prepare_weights(
        r,
        (
            r.radial,
            (r.environ_first, r.environ_second),
            (r.mixing_first, r.mixing_second),
            (r.coupler_first, r.coupler_second),
            r.readout,
        ),
        1.0 / math.sqrt(slots_per),
    )
    settle(0, copies)
    copies = leave(1)
    prepare_lists(r, r.neighbours)
    ghost_hot = hot_columns(r.ghosts[...], count)
    ghost_picks = ghost_hot.T.astype(bf16)
    ghost_hot = ghost_hot.astype(bf16)
    settle(1, copies)

    flat = holding[:, breadth:].astype(f32).T[:24]
    ghost_flat = product(flat.astype(bf16), ghost_hot)
    ghost_places = ghost_flat[:8] + ghost_flat[8:16] + ghost_flat[16:24]
    r.ghost_places[...] = ghost_places[:4]
    waits = {}
    for n in around:
        dx, dy = steps[n]
        waits[n] = [
            send(
                r.ghost_places,
                r.halo_places.at[n],
                (r.places_send.at[n], r.places_recv.at[n]),
                at(-dx, -dy),
            )
        ]
    rows = holding[:, :breadth]
    half_target = (0.5 * r.target_weight[...].astype(f32)).astype(bf16)
    half_source = (0.5 * r.source_weight[...].astype(f32)).astype(bf16)
    target = product(rows, half_target).astype(bf16)
    chunks = [pl.ds(c * (ghost_count // 2), ghost_count // 2) for c in range(2)]

    def send_rows(source, n, c, device):
        return send(
            source.at[chunks[c]],
            r.halo_rows.at[n, chunks[c]],
            (r.rows_send.at[n, c], r.rows_recv.at[n, c]),
            device,
        )

    cross = {}
    for c in range(2):
        part = slice(c * (ghost_count // 2), (c + 1) * (ghost_count // 2))
        r.ghost_rows[part] = product(ghost_picks[part], target).astype(bf16)
        for n in (1, 7):
            cross[n, c] = send_rows(r.ghost_rows, n, c, at(-steps[n][0], 0))
    for c in range(2):
        for n in (3, 5):
            waits[n].append(send_rows(r.ghost_rows, n, c, at(0, -steps[n][1])))

    r.table[:count, :] = target.astype(f32)
    r.source[...] = product(rows, half_source).astype(bf16).astype(f32)
    mine = flat[:8] + flat[8:16] + flat[16:24]
    r.own[...] = mine
    place = r.place
    place[...] = jnp.zeros(place.shape, f32)
    for k in range(3):
        for g in range(own_groups):
            place[k, g : g + 1, :] = mine[k : k + 1, g * breadth : (g + 1) * breadth]
    rows_at = pl.ds(count + 4 * ghost_count, ghost_count)
    r.table[rows_at, :] = jnp.zeros((ghost_count, breadth), f32)

    r.give[...] = jnp.zeros(r.give.shape, f32)
    for c in range(2):
        for n in (1, 7):
            cross[n, c].wait()
            for dy in (-1, 1):
                waits[n + dy].append(send_rows(r.halo_rows.at[n], n + dy, c, at(0, -dy)))
    for n in around:
        waits[n][0].wait()
        places = r.halo_places[n]
        for k in range(3):
            for g in range(ghost_groups):
                group = own_groups + n * ghost_groups + g
                place[k, group : group + 1, :] = places[
                    k : k + 1, g * breadth : (g + 1) * breadth
                ]
    prepare_places(r, place)
    geometry(r, r.own, basis, slots_per)
    spread_tiles(r)
    for copy in lists:
        copy.wait()
    for n in around:
        for copy in waits[n][1:]:
            copy.wait()
        rows_at = pl.ds(count + n * ghost_count, ghost_count)
        r.table[rows_at, :] = r.halo_rows[n].astype(f32)

    main_loop(r, r.table, r.source, slots_per, width, blocks)
    finish(r, r.scatter, basis)

    scatter = r.scatter
    groups = scatter.shape[0] // 3
    for n in range(9):
        for g in range(ghost_groups):
            group = own_groups + n * ghost_groups + g
            for k in range(3):
                r.give[n, k : k + 1, g * breadth : (g + 1) * breadth] = scatter[
                    pl.ds(k * groups + group, 1), :
                ]
    copies = {}
    for n in around:
        copies[n] = send(
            r.give.at[n], r.got.at[n], (r.give_send.at[n], r.give_recv.at[n]),
            at(*steps[n]),
        )
    gather_atoms(r, r.by_atom, r.energy, slots_per)
    spots = hot_columns(r.ghosts[...], count).T.astype(bf16)
    owns = []
    for k in range(3):
        own = jnp.concatenate(
            [scatter[pl.ds(k * groups + g, 1), :] for g in range(own_groups)], axis=1
        )
        owns.append(own + r.by_atom[k : k + 1, :])
    total = r.give[4][:3]
    for n in around:
        copies[n].wait()
        total = total + r.got[n][:3]
    stack = jnp.concatenate(
        [jnp.concatenate([x, jnp.zeros((5, ghost_count), f32)], axis=0) for x in split_three(total)],
        axis=0,
    ).astype(bf16)
    back = product(stack, spots)
    back = back[:8] + back[8:16] + back[16:24]
    for k in range(3):
        r.force[k] = -(owns[k] + back[k : k + 1, :])


def per_device(
    shape,
    features,
    coords,
    migrate_x_slots,
    migrate_y_slots,
    ghost_slots,
    neighbours,
    source_weight,
    target_weight,
    radial_weight,
    environ_first,
    mixing_first,
    coupler_first,
    environ_second,
    mixing_second,
    coupler_second,
    readout,
):
    features = features[0, 0]
    count, breadth = features.shape
    coords = coords.transpose(0, 2, 1, 3).reshape(3, 1, count)
    neighbours = neighbours[0, 0].T
    ghosts = ghost_slots.reshape(1, -1)
    slots_per = neighbours.shape[0]
    ghost_count = ghosts.shape[1]
    sent = migrate_x_slots.shape[3]
    total_rows = count + 9 * ghost_count
    groups = -(-(total_rows // breadth) // 8) * 8
    width, blocks = 4, 4
    vmem = pl.BlockSpec(memory_space=pltpu.VMEM)
    hbm = pl.BlockSpec(memory_space=pltpu.HBM)
    dma = pltpu.SemaphoreType.DMA
    square = pltpu.VMEM((breadth, breadth), bf16)
    inputs = dict(
        features_far=features,
        coords_far=coords,
        slots_x_far=migrate_x_slots[0, 0],
        slots_y_far=migrate_y_slots[0, 0],
        ghosts_far=ghosts,
        neighbours_far=neighbours,
        source_weight_far=source_weight,
        target_weight_far=target_weight,
        radial_far=radial_weight,
        environ_first_far=environ_first,
        mixing_first_far=mixing_first,
        coupler_first_far=coupler_first,
        environ_second_far=environ_second,
        mixing_second_far=mixing_second,
        coupler_second_far=coupler_second,
        readout_far=readout[None],
    )
    scratch = dict(
        features=pltpu.VMEM((count, breadth), bf16),
        slots_x=pltpu.VMEM((2, sent), jnp.int32),
        slots_y=pltpu.VMEM((2, sent), jnp.int32),
        ghosts=pltpu.VMEM((1, ghost_count), jnp.int32),
        source_weight=square,
        target_weight=square,
        radial=pltpu.VMEM(radial_weight.shape, f32),
        readout=pltpu.VMEM((1, breadth), bf16),
        environ_first=square,
        mixing_first=square,
        coupler_first=square,
        environ_second=square,
        mixing_second=square,
        coupler_second=square,
        coords=pltpu.VMEM((3, 1, count), f32),
        neighbours=pltpu.VMEM((slots_per, count), jnp.int32),
        fetch_sem=dma((8,)),
        index_sem=dma((slots_per,)),
        later_sem=dma((8,)),
        table=pltpu.VMEM((total_rows, breadth), f32),
        source=pltpu.VMEM((count, breadth), f32),
        place=pltpu.VMEM((3, groups, breadth), f32),
        own=pltpu.VMEM((8, count), f32),
        scatter=pltpu.VMEM((3 * groups, breadth), f32),
        by_atom=pltpu.VMEM((8, count), f32),
        holding=pltpu.VMEM((count, 2 * breadth), bf16),
        leaving=pltpu.VMEM((2, 2, sent, 2 * breadth), bf16),
        arriving=pltpu.VMEM((2, 2, sent, 2 * breadth), bf16),
        ghost_rows=pltpu.VMEM((ghost_count, breadth), bf16),
        ghost_places=pltpu.VMEM((4, ghost_count), f32),
        halo_rows=pltpu.VMEM((9, ghost_count, breadth), bf16),
        halo_places=pltpu.VMEM((9, 4, ghost_count), f32),
        give=pltpu.VMEM((9, 4, ghost_count), f32),
        got=pltpu.VMEM((9, 4, ghost_count), f32),
        move_send=dma((2, 2)),
        move_recv=dma((2, 2)),
        rows_send=dma((9, 2)),
        rows_recv=dma((9, 2)),
        places_send=dma((9,)),
        places_recv=dma((9,)),
        give_send=dma((9,)),
        give_recv=dma((9,)),
        **edge_scratch(count, slots_per, breadth, groups, width, blocks),
    )
    names = tuple(inputs) + ("force", "energy") + tuple(scratch)
    forces, energies = pl.pallas_call(
        functools.partial(whole_kernel, shape, (width, blocks), names),
        out_shape=(
            jax.ShapeDtypeStruct((3, 1, count), f32),
            jax.ShapeDtypeStruct((1, count), f32),
        ),
        in_specs=[hbm] * len(inputs),
        out_specs=(vmem,) * 2,
        scratch_shapes=list(scratch.values()),
        compiler_params=pltpu.CompilerParams(
            collective_id=0, has_side_effects=True, vmem_limit_bytes=67043328
        ),
        name="allegro",
    )(*inputs.values())
    return (forces.reshape(1, 3, 1, count).transpose(0, 2, 1, 3), energies[None])


def solution(mesh):
    in_specs = (
        P("gx", "gy", None, None),
        P("gx", "gy", None, None),
        P("gx", "gy", None, None),
        P("gx", "gy", None, None),
        P("gx", "gy", None),
        P("gx", "gy", None, None),
        P(),
        P(),
        P(),
        P(),
        P(),
        P(),
        P(),
        P(),
        P(),
        P(),
    )
    out_specs = (P("gx", "gy", None, None), P("gx", "gy", None))
    return jax.shard_map(
        functools.partial(per_device, (mesh.shape["gx"], mesh.shape["gy"])),
        mesh=mesh, in_specs=in_specs, out_specs=out_specs, check_vma=False
    )
```
